32 devices in a mesh: dp: 4 (over x, core), expert: 8 (over z, y).
Axes of the slice: x: 2, y: 2, z: 4, core: 2. Of those that a mesh axis runs over, the one named last changes fastest.
Arguments:
- tokens: bfloat16 [320, 4096], P('expert', 'dp'), may hold values from -6 to 6
- expert_ids: int32 [320, 8], P('expert'), may hold values from 0 to 15, all different within a row; in each aligned block of 320 rows (0 to 319, 320 to 639, ...) at most 240 rows name the same one
- routing_weights: bfloat16 [320, 8], P('expert'), may hold values from 0.049804688 to 0.29882812
- gate_weight: bfloat16 [16, 768, 4096], P('expert', None, 'dp'), may hold values from -0.09375 to 0.09375
- up_weight: bfloat16 [16, 768, 4096], P('expert', None, 'dp'), may hold values from -0.09375 to 0.09375
- down_weight: bfloat16 [16, 768, 4096], P('expert', None, 'dp'), may hold values from -0.21875 to 0.21875
- out_grad: bfloat16 [320, 4096], P('expert', 'dp'), may hold values from -1.5 to 1.5
Outputs:
- layer_out: bfloat16 [320, 4096], P('expert', 'dp')
- tokens_grad: bfloat16 [320, 4096], P('expert', 'dp')
- routing_grad: float32 [320, 8], P('expert')
- gate_weight_grad: bfloat16 [16, 768, 4096], P('expert', None, 'dp')
- up_weight_grad: bfloat16 [16, 768, 4096], P('expert', None, 'dp')
- down_weight_grad: bfloat16 [16, 768, 4096], P('expert', None, 'dp')
The draws below stay inside these ranges and needn't reach their ends.
Inputs may be any that keep to these rules, and one draw needn't show every extreme that they name: `expert_ids`: each row names 8 different experts. No expert is named by more than 240 rows, a bound that some block reaches.
All inputs are finite; a program needn't handle non-finite values.
Results may differ from the reference program's by a relative error of at most 0.02.
Values may be sent and summed in bfloat16 or wider, within the bound.
A program may use at most 128 MiB of HBM per device.

```python
import math
import jax
import jax.numpy as jnp
import numpy as np
from jax import lax

D = 4096
FF = 768
TOP = 8
EXP_DEV = 2
EXPERTS = 16
TOKENS = 320
CAP = 240
N_DP = 4
N_EXPERT = 8


def shard_levels(own_key, extent, pieces, smallest, largest):
    loudness = 1.0
    for dim, blocks in pieces:
        steps = jax.random.uniform(jax.random.fold_in(jax.random.fold_in(own_key, 6), dim), (blocks,), jnp.float32, smallest / len(pieces), largest / len(pieces))
        loudness = loudness * jnp.repeat(jnp.exp(steps), extent[dim] // blocks).reshape((-1,) + (1,) * (len(extent) - 1 - dim))
    return loudness


def deal_out(own_key, own, number, rows, count, top, most, slope):
    order = jax.random.permutation(own_key, count)
    crowded, ordinary = shares(count, rows * top, most, slope, True), shares(count, rows * top, most, slope, False)
    places = jnp.arange(count)

    def named(lengths, offset_by):
        used = int((lengths > 0).sum())
        fixed = max(1, used // 4)
        shifted = fixed + (places - fixed + offset_by * (used - fixed)) % max(1, count - fixed)
        return jnp.zeros((count,), jnp.int32).at[order[jnp.where(places < fixed, places, shifted)]].set(jnp.asarray(lengths, jnp.int32))

    lengths = jnp.where(number % 4 == 0, named(crowded, number // 4), named(ordinary, number - number // 4 - 1))
    mixed = jax.random.permutation(jax.random.fold_in(own, 3), count)
    giver, receiver = mixed[0:count // 2 * 2:2], mixed[1:count // 2 * 2:2]
    slack = jnp.minimum(lengths[giver] - 1, most - lengths[receiver]) // 2
    slack = jnp.where((giver == order[0]) | (receiver == order[0]) | (lengths[receiver] == 0), 0, jnp.maximum(slack, 0))
    shifted = jax.random.randint(jax.random.fold_in(own, 4), (count // 2,), 0, 1 << 20) % (slack + 1)
    lengths = lengths.at[giver].add(-shifted).at[receiver].add(shifted)
    items = jnp.searchsorted(jnp.cumsum(lengths), jnp.arange(rows * top), side="right").astype(jnp.int32)
    listing = items.reshape(top, rows).T
    listing = listing[jax.random.permutation(jax.random.fold_in(own, 1), rows)]
    offset_by = jax.random.randint(jax.random.fold_in(own, 2), (rows, 1), 0, top)
    return jnp.take_along_axis(listing, (jnp.arange(top)[None, :] + offset_by) % top, axis=1)


def shares(count, total, reach, lean, full):
    weights = [(1 << 20) // math.isqrt(rank ** lean) + 1 for rank in range(1, count + 1)]
    largest = reach if full else min(reach, max(-(-total // count), total * weights[0] // sum(weights)))
    least = 1 if total - largest >= count - 1 else 0
    holding, rest = [largest] + [least] * (count - 1), total - largest - least * (count - 1)
    while rest > 0:
        candidates = [i for i in range(1, count) if holding[i] < largest] or [i for i in range(1, count) if holding[i] < reach]
        mass, left = sum([weights[i] for i in candidates]), rest
        for i in candidates:
            extra = min(reach - holding[i], max(1, left * weights[i] // mass), rest)
            holding[i] = holding[i] + extra
            rest = rest - extra
    return np.array(holding)


def normal_values(own_key, extent, deviation, most, pieces=(), kind=jnp.bfloat16):
    level = shard_levels(own_key, extent, pieces, -0.22, 0.18) if pieces else 1.0
    result = jax.random.normal(own_key, extent, jnp.float32) * deviation * level
    return jnp.minimum(jnp.maximum(result, -most), most).astype(kind)


def setup_inputs(seed: int = 0) -> dict:
    keys = jax.random.split(jax.random.key(seed), 8)
    tokens = normal_values(keys[0], (TOKENS, D), 1.0, 6.0, ((0, 8), (1, 4)))
    expert_ids_keys = jax.random.split(jax.random.fold_in(keys[1], 1), TOKENS // TOKENS)
    expert_ids_turns = jax.random.permutation(jax.random.fold_in(keys[1], 3), TOKENS // TOKENS)
    expert_ids = jax.vmap(lambda own, number: deal_out(jax.random.fold_in(keys[1], 2), own, number, TOKENS, EXPERTS, TOP, CAP, 2))(expert_ids_keys, expert_ids_turns).reshape((TOKENS, TOP))
    routing_weights = jnp.clip(0.049804688 + 0.24902344 * jax.random.uniform(keys[2], (TOKENS, TOP), jnp.float32) ** shard_levels(keys[2], (TOKENS, TOP), ((0, 8),), -0.2, 0.2), 0.049804688, 0.29882812).astype(jnp.bfloat16)
    gate_weight = normal_values(keys[3], (EXPERTS, FF, D), D ** -0.5, 0.09375, ((0, 8), (2, 4)))
    up_weight = normal_values(keys[4], (EXPERTS, FF, D), D ** -0.5, 0.09375, ((0, 8), (2, 4)))
    down_weight = normal_values(keys[5], (EXPERTS, FF, D), FF ** -0.5, 0.21875, ((0, 8), (2, 4)))
    out_grad = normal_values(keys[6], (TOKENS, D), 0.25, 1.5, ((0, 8), (1, 4)))
    return dict(tokens=tokens, expert_ids=expert_ids, routing_weights=routing_weights, gate_weight=gate_weight, up_weight=up_weight, down_weight=down_weight, out_grad=out_grad)


def build_lists(flat_ids, expert):
    matches = flat_ids == expert
    rank_pos = jnp.cumsum(matches.astype(jnp.int32), dtype=jnp.int32) - 1
    target_pos = jnp.where(matches, rank_pos, CAP).astype(jnp.int32)
    slot_ids = jnp.arange(flat_ids.shape[0], dtype=jnp.int32)
    slot_lists = jnp.zeros((CAP,), jnp.int32).at[target_pos].set(slot_ids, mode="drop")
    total = jnp.sum(matches.astype(jnp.int32), dtype=jnp.int32)
    is_live = jnp.arange(CAP, dtype=jnp.int32) < total
    return slot_lists, is_live


def grouped_sum(left, right):
    group_width = D // N_DP
    parts = jnp.einsum("rjd,fjd->jrf", left.reshape(CAP, N_DP, group_width).astype(jnp.float32),
                       right.reshape(right.shape[0], N_DP, group_width).astype(jnp.float32))
    parts = lax.optimization_barrier(parts.astype(jnp.bfloat16))
    return jnp.sum(parts.astype(jnp.float32), axis=0)


def reference(tokens, expert_ids, routing_weights, gate_weight, up_weight, down_weight, out_grad):
    flat_ids = expert_ids.reshape(-1)
    flat_weights = routing_weights.reshape(-1).astype(jnp.float32)
    group_width = D // N_DP

    def one_group(carry, inputs):
        out_sum, input_sum, weight_sum = carry
        group, gate_set, up_set, down_set = inputs
        group_out = jnp.zeros((TOKENS, D), jnp.float32)
        group_in = jnp.zeros((TOKENS, D), jnp.float32)
        gate_list, up_list, down_list = [], [], []
        for local in range(EXP_DEV):
            expert = (group * EXP_DEV + local).astype(jnp.int32)
            w_gate, w_up, w_down = gate_set[local], up_set[local], down_set[local]
            slot_lists, is_live = build_lists(flat_ids, expert)
            token_index = (slot_lists // TOP).astype(jnp.int32)
            live_rows = is_live.astype(jnp.float32)
            row_acts = jnp.where(is_live[:, None], tokens[token_index], jnp.zeros((), jnp.bfloat16))
            gate_pre = grouped_sum(row_acts, w_gate)
            up_pre = grouped_sum(row_acts, w_up)
            hidden = (jax.nn.silu(gate_pre) * up_pre).astype(jnp.bfloat16)
            expert_out = jnp.dot(hidden, w_down, preferred_element_type=jnp.float32)
            row_scale = flat_weights[slot_lists] * live_rows
            group_out = group_out.at[token_index].add(expert_out * row_scale[:, None])
            grad_rows = out_grad[token_index].astype(jnp.float32)
            dot_groups = jnp.sum((grad_rows * expert_out).reshape(CAP, N_DP, group_width), axis=2)
            dot_groups = lax.optimization_barrier(dot_groups.astype(jnp.bfloat16))
            dots = jnp.sum(dot_groups.astype(jnp.float32), axis=1) * live_rows
            weight_sum = weight_sum.at[slot_lists].add(dots)
            scaled_grad = (grad_rows * row_scale[:, None]).astype(jnp.bfloat16)
            hidden_grad = grouped_sum(scaled_grad, w_down)
            gate_sig = jax.nn.sigmoid(gate_pre)
            gate_delta = (hidden_grad * up_pre * gate_sig * (1.0 + gate_pre * (1.0 - gate_sig))).astype(jnp.bfloat16)
            up_delta = (hidden_grad * gate_pre * gate_sig).astype(jnp.bfloat16)
            down_list.append(jnp.dot(hidden.T, scaled_grad, preferred_element_type=jnp.float32).astype(jnp.bfloat16))
            gate_list.append(jnp.dot(gate_delta.T, row_acts, preferred_element_type=jnp.float32).astype(jnp.bfloat16))
            up_list.append(jnp.dot(up_delta.T, row_acts, preferred_element_type=jnp.float32).astype(jnp.bfloat16))
            row_grad = jnp.dot(gate_delta, w_gate, preferred_element_type=jnp.float32)
            row_grad = row_grad + jnp.dot(up_delta, w_up, preferred_element_type=jnp.float32)
            group_in = group_in.at[token_index].add(row_grad)
        out_sum = out_sum + lax.optimization_barrier(group_out.astype(jnp.bfloat16)).astype(jnp.float32)
        input_sum = input_sum + lax.optimization_barrier(group_in.astype(jnp.bfloat16)).astype(jnp.float32)
        return (out_sum, input_sum, weight_sum), (jnp.stack(gate_list), jnp.stack(up_list), jnp.stack(down_list))

    start = (jnp.zeros((TOKENS, D), jnp.float32), jnp.zeros((TOKENS, D), jnp.float32),
             jnp.zeros((TOKENS * TOP,), jnp.float32))
    groups_all = jnp.arange(N_EXPERT, dtype=jnp.int32)
    (out_sum, input_sum, weight_sum), (gate_grads, up_grads, down_grads) = lax.scan(
        one_group, start,
        (groups_all, gate_weight.reshape(N_EXPERT, EXP_DEV, FF, D), up_weight.reshape(N_EXPERT, EXP_DEV, FF, D),
         down_weight.reshape(N_EXPERT, EXP_DEV, FF, D)))
    return (out_sum.astype(jnp.bfloat16), input_sum.astype(jnp.bfloat16), weight_sum.reshape(TOKENS, TOP),
            gate_grads.reshape(EXPERTS, FF, D), up_grads.reshape(EXPERTS, FF, D), down_grads.reshape(EXPERTS, FF, D))
```

```python
import functools
import jax
import jax.numpy as jnp
from jax import lax
from jax.experimental import pallas as pl
from jax.experimental.pallas import tpu as pltpu
from jax.sharding import PartitionSpec as P

CAP = 240
F32 = jnp.float32
BF = jnp.bfloat16
VM = pl.BlockSpec(memory_space=pltpu.VMEM)
ANY = pl.BlockSpec(memory_space=pl.ANY)
MESH = pl.DeviceIdType.MESH


def up_to(x, k):
    return (x + k - 1) // k * k


def factor(n):
    slow = 4 if n % 4 == 0 else 1
    return slow, n // slow


def flip(a, j):
    bit = 1
    while bit <= j:
        if j & bit:
            a = a + bit - 2 * bit * lax.rem(a // bit, 2)
        bit *= 2
    return a


def remote(src, dst, send, recv, where):
    return pltpu.make_async_remote_copy(
        src_ref=src, dst_ref=dst, send_sem=send, recv_sem=recv,
        device_id=where, device_id_type=MESH,
    )


def dotted(x, y, dx, dy):
    return lax.dot_general(x, y, (((dx,), (dy,)), ((), ())), preferred_element_type=F32)


class Plan:
    def __init__(self, n, nd, tb, top, e, f, d):
        self.n, self.nd, self.tb, self.top, self.e, self.f, self.d = n, nd, tb, top, e, f, d
        self.slow, self.fast = factor(n)
        self.m = nd // 2
        self.h = e // 2
        self.experts = n * e
        self.tbp = up_to(tb, 16)
        self.tl = up_to(n * self.tbp, 128)
        order = list(range(self.slow))
        self.zorder = order[0::2] + order[1::2]
        self.nz = max(1, self.slow // 2)
        self.early = self.zorder[:self.nz]
        self.late = self.zorder[self.nz:]
        self.hb = self.nz * self.fast * self.tbp
        n1 = self.nz * self.fast * tb
        n2 = n * tb - n1
        lo = max(0, CAP - n2) // 16 * 16
        hi = min(CAP, up_to(n1, 16))
        self.hi = hi
        spans = []
        half = up_to(self.hb, 128)
        back = self.hb // 128 * 128
        for s0, s1, l0, l1, needs_late in ((0, lo, 0, half, False), (lo, hi, 0, self.tl, True),
                                           (hi, CAP, back, self.tl, True)):
            if s1 > s0:
                spans.append((s0, s1, l0, l1, needs_late))
        self.spans = spans
        self.lo = lo
        self.half, self.back = half, back

    def place(self, jz, jj):
        return self.zorder.index(jz) * self.fast + jj


def main_kernel(p, tok_h, grad_h, ids, wts, gw_h, uw_h, dw_h,
                layer_o, tgrad_o, rg_o, hid, gd, ud, rows, sgrad,
                gw, uw, dw, tokb, gradb, tokf, gradf, wown, wall, one, scaled, grows,
                psend, precv, mine, got, eb, terms, dmat, osend, isend, dsend,
                orb, irb, drb, oacc, iacc, dacc, ozb, izb, dzb, dots,
                wsem, lsem, ms, mr, zs, zr, ys, yr, ps, pr, xs, xr, hs, hr,
                rys, ryr, rzs, rzr, ds_, dr_):
    n, nd, tb, e, f, d = p.n, p.nd, p.tb, p.e, p.f, p.d
    slow, fast, m, h, tbp = p.slow, p.fast, p.m, p.h, p.tbp
    me = lax.axis_index("expert")
    dp = lax.axis_index("dp")
    a, b = me // fast, lax.rem(me, fast)
    chip, core = dp // 2, lax.rem(dp, 2)
    partner = {"dp": chip * 2 + 1 - core}
    spans = p.spans
    nc = len(spans)

    loads = [pltpu.make_async_copy(x, y, wsem.at[i]) for i, (x, y) in enumerate(((gw_h, gw), (uw_h, uw), (dw_h, dw)))]
    mine_in = [pltpu.make_async_copy(x, y.at[me], lsem.at[i]) for i, (x, y) in enumerate(((tok_h, tokb), (grad_h, gradb)))]
    for c in mine_in + loads:
        c.start()

    which = lax.broadcasted_iota(jnp.int32, (p.experts, tb), 0)
    w = jnp.zeros((p.experts, tb), F32)
    for k in range(p.top):
        w = w + jnp.where(which == ids[k:k + 1, :], wts[k:k + 1, :].astype(F32), 0.0)
    wown[...] = jnp.zeros_like(wown)
    wown[:, 0:tb] = w.astype(BF)
    wall[me] = wown[...]

    sem = pltpu.get_barrier_semaphore()
    for j in range(1, n):
        pl.semaphore_signal(sem, inc=1, device_id={"expert": lax.rem(me + j, n)}, device_id_type=MESH)
    for j in range(1, nd):
        pl.semaphore_signal(sem, inc=1, device_id={"dp": lax.rem(dp + j, nd)}, device_id_type=MESH)
    pl.semaphore_wait(sem, n - 1 + nd - 1)

    blocks, homes = (tokb, gradb), (tok_h, grad_h)

    def source(jz, jj):
        return flip(a, jz) * fast + lax.rem(b - jj + fast, fast)

    def meta(j):
        return remote(wown, wall.at[me], ms.at[j], mr.at[j], {"expert": lax.rem(me + j, n)})

    def zcopy(i, jz):
        return remote(homes[i], blocks[i].at[me], zs.at[i, jz], zr.at[i, jz], {"expert": flip(a, jz) * fast + b})

    def ycopy(i, jz, jj):
        blk = source(jz, 0)
        src = homes[i] if jz == 0 else blocks[i].at[blk]
        return remote(src, blocks[i].at[blk], ys.at[i, jz, jj], yr.at[i, jz, jj],
                      {"expert": a * fast + lax.rem(b + jj, fast)})

    def forward(i, jz):
        if jz:
            zcopy(i, jz).wait_recv()
        for jj in range(1, fast):
            ycopy(i, jz, jj).start()

    def spread(i):
        for jz in p.zorder:
            if jz:
                zcopy(i, jz).start()
        forward(i, 0)

    def settle(i, group, flat):
        for jz in group:
            for jj in range(fast):
                if jj:
                    ycopy(i, jz, jj).wait_recv()
                elif jz == 0:
                    mine_in[i].wait()
                at = p.place(jz, jj) * tbp
                flat[at:at + tb] = blocks[i][source(jz, jj)]

    def late_of(i):
        for jz in p.late:
            forward(i, jz)

    for j in range(1, n):
        meta(j).start()
    spread(0)

    tokf[...] = jnp.zeros_like(tokf)
    gradf[...] = jnp.zeros_like(gradf)
    tl = p.tl
    lower = ((lax.broadcasted_iota(jnp.int32, (tl, tl), 0) < lax.broadcasted_iota(jnp.int32, (tl, tl), 1))
             & ((lax.broadcasted_iota(jnp.int32, (tl, tl), 0) < p.hb)
                == (lax.broadcasted_iota(jnp.int32, (tl, tl), 1) < p.hb)))
    lower = jnp.where(lower, 1.0, 0.0).astype(BF)

    for jz in p.early:
        if jz:
            forward(0, jz)
    for j in range(1, n):
        meta(j).wait_recv()

    sub = lax.broadcasted_iota(jnp.int32, (p.experts, 128), 0)
    row = lax.broadcasted_iota(jnp.int32, (16, 128), 0)
    wl = jnp.zeros((16, tl), F32)
    for jz in p.zorder:
        for jj in range(fast):
            full = wall[source(jz, jj)].astype(F32)
            v = jnp.zeros((16, 128), F32)
            for i in range(e):
                v = jnp.where(row == i, jnp.sum(jnp.where(sub == me * e + i, full, 0.0), axis=0, keepdims=True), v)
            if tl > 128:
                v = jnp.concatenate([v, jnp.zeros((16, tl - 128), F32)], axis=1)
            at = p.place(jz, jj) * tbp
            wl = wl + (pltpu.roll(v, at, 1) if at else v)
    match = wl > 0.0
    rank = dotted(jnp.where(match, 1.0, 0.0).astype(BF), lower, 1, 0)
    lane = lax.broadcasted_iota(jnp.int32, (16, tl), 1)
    at_slot = jnp.where(match, jnp.where(lane < p.hb, rank, CAP - 1.0 - rank), -1.0)
    line = lax.broadcasted_iota(jnp.int32, (CAP, tl), 0).astype(F32)
    for i in range(e):
        pick = jnp.abs(line - at_slot[i:i + 1, :]) < 0.5
        one[i] = jnp.where(pick, 1.0, 0.0).astype(BF)
        scaled[i] = jnp.where(pick, wl[i:i + 1, :], 0.0).astype(BF)

    settle(0, p.early, tokf)

    def take(table, flat, out, c):
        s0, s1, l0, l1, _ = spans[c]
        for i in range(e):
            out[i, s0:s1] = dotted(table[i, s0:s1, l0:l1], flat[l0:l1], 1, 0).astype(BF)

    def product(k, i, c):
        s0, s1 = spans[c][:2]
        left = (rows, rows, sgrad)[k]
        right = (gw, uw, dw)[k]
        return dotted(left[i, s0:s1], right[i], 1, 1)

    def pair(k, c):
        s0, s1 = spans[c][:2]
        return remote(psend.at[k, :, s0:s1], precv.at[k, :, s0:s1], ps.at[k, c], pr.at[k, c], partner)

    def cross(k, c, j):
        s0, s1 = spans[c][:2]
        return remote(mine.at[k, :, s0:s1], got.at[k, j, :, s0:s1], xs.at[k, c, j], xr.at[k, c, j],
                      {"dp": lax.rem(chip + j, m) * 2 + core})

    def theirs(k, c):
        s0, s1 = spans[c][:2]
        for u in range(h):
            psend[k, u, s0:s1] = product(k, (1 - core) * h + u, c).astype(BF)
        pair(k, c).start()

    def ours(k, c):
        s0, s1 = spans[c][:2]
        part = [product(k, core * h + u, c) for u in range(h)]
        pair(k, c).wait_recv()
        for u in range(h):
            mine[k, u, s0:s1] = (part[u] + precv[k, u, s0:s1].astype(F32)).astype(BF)
        for j in range(1, m):
            cross(k, c, j).start()

    def total(k, c, u):
        s0, s1 = spans[c][:2]
        v = mine[k, u, s0:s1].astype(F32)
        for j in range(1, m):
            v = v + got[k, j, u, s0:s1].astype(F32)
        return v

    def share(k, c):
        s0, s1 = spans[c][:2]
        full = (hid, gd, ud)[k]
        view = full.at[pl.ds(core * h, h), s0:s1]
        return remote(view, view, hs.at[k, c], hr.at[k, c], partner)

    def make_hidden(c):
        s0, s1 = spans[c][:2]
        for k in (0, 1):
            for j in range(1, m):
                cross(k, c, j).wait_recv()
        for u in range(h):
            gate, up = total(0, c, u), total(1, c, u)
            hid[core * h + u, s0:s1] = (gate * jax.nn.sigmoid(gate) * up).astype(BF)
        share(0, c).start()

    def make_delta(c):
        s0, s1 = spans[c][:2]
        for j in range(1, m):
            cross(2, c, j).wait_recv()
        for u in range(h):
            gate, up, hg = total(0, c, u), total(1, c, u), total(2, c, u)
            sig = jax.nn.sigmoid(gate)
            gd[core * h + u, s0:s1] = (hg * up * sig * (1.0 + gate * (1.0 - sig))).astype(BF)
            ud[core * h + u, s0:s1] = (hg * gate * sig).astype(BF)
        share(1, c).start()
        share(2, c).start()

    first = [c for c in range(nc) if not spans[c][4]]
    rest = [c for c in range(nc) if spans[c][4]]
    for i in range(2):
        loads[i].wait()
    for c in first:
        take(one, tokf, rows, c)
        theirs(0, c)
        theirs(1, c)
    late_of(0)
    for c in first:
        ours(0, c)
        ours(1, c)
    settle(0, p.late, tokf)
    spread(1)
    for c in rest:
        take(one, tokf, rows, c)
        theirs(0, c)
        theirs(1, c)
        ours(0, c)
        ours(1, c)
    for jz in p.zorder:
        if jz:
            forward(1, jz)
    settle(1, p.zorder, gradf)
    loads[2].wait()
    for c in range(nc):
        take(scaled, gradf, sgrad, c)
        theirs(2, c)
        take(one, gradf, grows, c)
        ours(2, c)

    def back(table, i, s0, s1, l0, l1, x):
        return dotted(table[i, s0:s1, l0:l1], x, 0, 0)

    sends = (osend, isend, dsend)
    rbufs = (orb, irb, drb)
    accs = (oacc, iacc, dacc)
    zbufs = (ozb, izb, dzb)

    def ry(i, jz, jj):
        to = a * fast + lax.rem(b + jj, fast)
        return remote(sends[i].at[flip(a, jz) * fast + lax.rem(b + jj, fast)], rbufs[i].at[jz, jj],
                      rys.at[i, jz, jj], ryr.at[i, jz, jj], {"expert": to})

    def rz(i, jz):
        return remote(accs[i].at[jz], zbufs[i].at[jz], rzs.at[i, jz], rzr.at[i, jz],
                      {"expert": flip(a, jz) * fast + b})

    def reply(jz, jj):
        return flip(a, jz) * fast + lax.rem(b + jj, fast)

    def lanes_of(group):
        if group is p.early:
            return 0, p.half, 0
        return p.back, p.tl, p.hb - p.back

    def put(i, group, value, skip, c0, c1):
        for g, jz in enumerate(group):
            for jj in range(fast):
                at = skip + (g * fast + jj) * tbp
                sends[i][reply(jz, (fast - jj) % fast), :, c0:c1] = value[at:at + tb].astype(BF)

    db = 256 if d % 256 == 0 else d

    def expert_out(cs):
        s0, s1 = spans[cs[0]][0], spans[cs[-1]][1]
        for i in range(e):
            dot = jnp.zeros((s1 - s0, 1), F32)
            for c0 in range(0, d, db):
                v = dotted(hid[i, s0:s1], dw[i, :, c0:c0 + db], 1, 0)
                eb[i, s0:s1, c0:c0 + db] = v.astype(BF)
                dot = dot + jnp.sum(v * grows[i, s0:s1, c0:c0 + db].astype(F32), axis=1, keepdims=True)
            at = lax.broadcasted_iota(jnp.int32, (s1 - s0, dmat.shape[2]), 1) == me * e + i
            dmat[i, s0:s1] = jnp.where(at, dot, 0.0).astype(BF)

    def row_terms(cs):
        s0, s1 = spans[cs[0]][0], spans[cs[-1]][1]
        for i in range(e):
            for c0 in range(0, d, db):
                terms[i, s0:s1, c0:c0 + db] = (dotted(gd[i, s0:s1], gw[i, :, c0:c0 + db], 1, 0)
                                               + dotted(ud[i, s0:s1], uw[i, :, c0:c0 + db], 1, 0)).astype(BF)

    def send_sum(i, table, data, group):
        s0, s1 = (0, p.hi) if group is p.early else (p.lo, CAP)
        l0, l1, skip = lanes_of(group)
        for c0 in range(0, d, db):
            v = sum(back(table, x, s0, s1, l0, l1, data[x, s0:s1, c0:c0 + db]) for x in range(e))
            put(i, group, v, skip, c0, c0 + db)
        for jz in reversed(group):
            for jj in range(1, fast):
                ry(i, jz, jj).start()

    def send_dots(group):
        s0, s1 = (0, p.hi) if group is p.early else (p.lo, CAP)
        l0, l1, skip = lanes_of(group)
        v = sum(dotted(dmat[x, s0:s1], one[x, s0:s1, l0:l1], 0, 0) for x in range(e))
        v = v[:p.experts]
        width = l1 - l0
        for g, jz in enumerate(group):
            for jj in range(fast):
                at = skip + (g * fast + jj) * tbp
                sends[2][reply(jz, (fast - jj) % fast)] = (pltpu.roll(v, (width - at) % width, 1) if at else v)[:, :128].astype(BF)
        for jz in reversed(group):
            for jj in range(1, fast):
                ry(2, jz, jj).start()

    def pass_on(i, group):
        for jz in reversed(group):
            v = sends[i][flip(a, jz) * fast + b].astype(F32)
            for jj in range(1, fast):
                ry(i, jz, jj).wait_recv()
                v = v + rbufs[i][jz, jj].astype(F32)
            accs[i][jz] = v.astype(BF)
            if jz:
                rz(i, jz).start()

    def result(i):
        v = accs[i][0].astype(F32)
        for jz in range(1, slow):
            rz(i, jz).wait_recv()
            v = v + zbufs[i][jz].astype(F32)
        return v

    def share_recv(k, cs):
        for c in cs:
            share(k, c).wait_recv()

    near = [c for c in range(nc) if spans[c][0] < p.hi]
    far = [c for c in range(nc) if spans[c][0] >= p.hi]
    for c in near:
        make_hidden(c)
    share_recv(0, near)
    expert_out(near)
    send_sum(0, scaled, eb, p.early)
    send_dots(p.early)
    for c in far:
        make_hidden(c)
    if far:
        share_recv(0, far)
        expert_out(far)
    if p.late:
        send_sum(0, scaled, eb, p.late)
        send_dots(p.late)
    for c in near:
        make_delta(c)
    for i in (0, 2):
        pass_on(i, p.early)
    for k in (1, 2):
        share_recv(k, near)
    row_terms(near)
    send_sum(1, one, terms, p.early)
    for c in far:
        make_delta(c)
    if p.late:
        for i in (0, 2):
            pass_on(i, p.late)
    if far:
        for k in (1, 2):
            share_recv(k, far)
        row_terms(far)
    if p.late:
        send_sum(1, one, terms, p.late)
    pass_on(1, p.early)

    def across(j):
        return remote(dots.at[0], dots.at[j], ds_.at[j], dr_.at[j], {"dp": lax.rem(dp + j, nd)})

    dots[0] = result(2).astype(BF)
    for j in range(1, nd):
        across(j).start()
    if p.late:
        pass_on(1, p.late)
    layer_o[...] = result(0).astype(BF)
    v = dots[0].astype(F32)
    for j in range(1, nd):
        across(j).wait()
        v = v + dots[j].astype(F32)
    v = v[:, :tb]
    for k in range(p.top):
        rg_o[k:k + 1, :] = jnp.sum(jnp.where(which == ids[k:k + 1, :], v, 0.0), axis=0, keepdims=True)
    tgrad_o[...] = result(1).astype(BF)

    for j in range(1, n):
        meta(j).wait_send()
    for i in range(2):
        for jz in range(slow):
            if jz:
                zcopy(i, jz).wait_send()
            for jj in range(1, fast):
                ycopy(i, jz, jj).wait_send()
    for k in range(3):
        for c in range(nc):
            pair(k, c).wait_send()
            share(k, c).wait_send()
            for j in range(1, m):
                cross(k, c, j).wait_send()
    for i in range(3):
        for jz in range(slow):
            if jz:
                rz(i, jz).wait_send()
            for jj in range(1, fast):
                ry(i, jz, jj).wait_send()


def main_call(n, nd, tok, grad, ids, wts, gw, uw, dw):
    e, f, d = gw.shape
    tb, top = tok.shape[0], ids.shape[0]
    p = Plan(n, nd, tb, top, e, f, d)
    nc = len(p.spans)
    vm, dma = pltpu.VMEM, pltpu.SemaphoreType.DMA
    s = jax.ShapeDtypeStruct
    block, el = (tb, d), up_to(p.experts, 128)
    dot = (p.experts, 128)
    per_half = (p.h, CAP, f)
    return pl.pallas_call(
        functools.partial(main_kernel, p),
        out_shape=[s((tb, d), BF), s((tb, d), BF), s((top, tb), F32)] + [s((e, CAP, f), BF)] * 3 + [s((e, CAP, d), BF)] * 2,
        in_specs=[ANY, ANY, VM, VM, ANY, ANY, ANY],
        out_specs=[VM] * 8,
        scratch_shapes=[vm((e, f, d), BF)] * 3 + [vm((n,) + block, BF)] * 2 + [vm((p.tl, d), BF)] * 2
        + [vm(dot, BF), vm((n,) + dot, BF)] + [vm((e, CAP, p.tl), BF)] * 2 + [vm((e, CAP, d), BF)]
        + [vm((3,) + per_half, BF)] * 3 + [vm((3, p.m) + per_half, BF)]
        + [vm((e, CAP, d), BF)] * 2 + [vm((e, CAP, el), BF)]
        + [vm((n,) + block, BF)] * 2 + [vm((n,) + dot, BF)]
        + [vm((p.slow, p.fast) + block, BF)] * 2 + [vm((p.slow, p.fast) + dot, BF)]
        + ([vm((p.slow,) + block, BF)] * 2 + [vm((p.slow,) + dot, BF)]) * 2
        + [vm((nd,) + dot, BF)]
        + [dma((3,)), dma((2,))] + [dma((n,))] * 2 + [dma((2, p.slow))] * 2 + [dma((2, p.slow, p.fast))] * 2
        + [dma((3, nc))] * 2 + [dma((3, nc, p.m))] * 2 + [dma((3, nc))] * 2
        + [dma((3, p.slow, p.fast))] * 2 + [dma((3, p.slow))] * 2 + [dma((nd,))] * 2,
        compiler_params=pltpu.CompilerParams(collective_id=0, has_side_effects=True, vmem_limit_bytes=54 << 20),
    )(tok, grad, ids, wts, gw, uw, dw)


def weight_kernel(hid, gd, ud, rows, sgrad, layer, tgrad, rg, layer_o, tgrad_o, rg_o, gate_o, up_o, down_o):
    @pl.when((pl.program_id(0) == 0) & (pl.program_id(1) == 0))
    def _():
        layer_o[...] = layer[...]
        tgrad_o[...] = tgrad[...]
        rg_o[...] = rg[...]

    gate_o[0] = dotted(gd[0], rows[0], 0, 0).astype(BF)
    up_o[0] = dotted(ud[0], rows[0], 0, 0).astype(BF)
    down_o[0] = dotted(hid[0], sgrad[0], 0, 0).astype(BF)


def weight_grads(hidden, gd, ud, rows, sgrad, layer, tgrad, rg):
    e, c, f = hidden.shape
    d = rows.shape[2]
    fb = 256 if f % 256 == 0 else f
    narrow = pl.BlockSpec((1, c, fb), lambda i, j: (i, 0, j))
    whole = pl.BlockSpec((1, c, d), lambda i, j: (i, 0, 0))
    out = pl.BlockSpec((1, fb, d), lambda i, j: (i, j, 0))
    small = [pl.BlockSpec(x.shape, lambda i, j: (0, 0)) for x in (layer, tgrad, rg)]
    return pl.pallas_call(
        weight_kernel, grid=(e, f // fb),
        out_shape=[jax.ShapeDtypeStruct(x.shape, x.dtype) for x in (layer, tgrad, rg)]
        + [jax.ShapeDtypeStruct((e, f, d), BF)] * 3,
        in_specs=[narrow] * 3 + [whole] * 2 + small, out_specs=small + [out] * 3,
        compiler_params=pltpu.CompilerParams(vmem_limit_bytes=24 << 20),
    )(hidden, gd, ud, rows, sgrad, layer, tgrad, rg)


def body(n, nd, tokens, expert_ids, routing_weights, gate_weight, up_weight, down_weight, out_grad):
    layer, tgrad, rg, hid, gd, ud, rows, sgrad = main_call(
        n, nd, tokens, out_grad, expert_ids.T, routing_weights.T, gate_weight, up_weight, down_weight)
    layer, tgrad, rg, gate_grad, up_grad, down_grad = weight_grads(hid, gd, ud, rows, sgrad, layer, tgrad, rg)
    return layer, tgrad, rg.T, gate_grad, up_grad, down_grad


def solution(mesh):
    n, nd = mesh.shape["expert"], mesh.shape["dp"]
    w = P("expert", None, "dp")
    x = P("expert", "dp")
    r = P("expert", None)
    return jax.shard_map(functools.partial(body, n, nd), mesh=mesh, in_specs=(x, r, r, w, w, w, x),
                         out_specs=(x, x, r, w, w, w), check_vma=False)
```

```python
import functools
import jax
import jax.numpy as jnp
from jax import lax
from jax.experimental import pallas as pl
from jax.experimental.pallas import tpu as pltpu
from jax.sharding import PartitionSpec as P

CAP = 240
F32 = jnp.float32
BF = jnp.bfloat16
VM = pl.BlockSpec(memory_space=pltpu.VMEM)
ANY = pl.BlockSpec(memory_space=pl.ANY)
HBM = pl.BlockSpec(memory_space=pltpu.HBM)
MESH = pl.DeviceIdType.MESH


def up_to(x, k):
    return (x + k - 1) // k * k


def factor(n):
    slow = 4 if n % 4 == 0 else 1
    return slow, n // slow


def flip(a, j):
    bit = 1
    while bit <= j:
        if j & bit:
            a = a + bit - 2 * bit * lax.rem(a // bit, 2)
        bit *= 2
    return a


def remote(src, dst, send, recv, where):
    return pltpu.make_async_remote_copy(
        src_ref=src, dst_ref=dst, send_sem=send, recv_sem=recv,
        device_id=where, device_id_type=MESH,
    )


def dotted(x, y, dx, dy):
    return lax.dot_general(x, y, (((dx,), (dy,)), ((), ())), preferred_element_type=F32)


class Plan:
    def __init__(self, n, nd, tb, top, e, f, d):
        self.n, self.nd, self.tb, self.top, self.e, self.f, self.d = n, nd, tb, top, e, f, d
        self.slow, self.fast = factor(n)
        self.m = nd // 2
        self.h = e // 2
        self.experts = n * e
        self.tbp = up_to(tb, 16)
        self.tl = up_to(n * self.tbp, 128)
        order = list(range(self.slow))
        self.zorder = order[0::2] + order[1::2]
        self.nz = max(1, self.slow // 2)
        self.early = self.zorder[:self.nz]
        self.late = self.zorder[self.nz:]
        self.hb = self.nz * self.fast * self.tbp
        n1 = self.nz * self.fast * tb
        n2 = n * tb - n1
        lo = max(0, CAP - n2) // 16 * 16
        hi = min(CAP, up_to(n1, 16))
        self.hi = hi
        spans = []
        half = up_to(self.hb, 128)
        back = self.hb // 128 * 128
        for s0, s1, l0, l1, needs_late in ((0, lo, 0, half, False), (lo, hi, 0, self.tl, True),
                                           (hi, CAP, back, self.tl, True)):
            if s1 > s0:
                spans.append((s0, s1, l0, l1, needs_late))
        self.spans = spans
        self.lo = lo
        self.half, self.back = half, back

    def place(self, jz, jj):
        return self.zorder.index(jz) * self.fast + jj


def main_kernel(p, tok_h, grad_h, ids_h, wts_h, gw_h, uw_h, dw_h,
                layer_o, tgrad_o, rg_o, gate_o, up_o, down_o,
                ids, wts, hid, gd, ud, rows, sgrad, gw, uw, dw, tokb, gradb, tokf, gradf, wown, wall, one, scaled, grows,
                psend, precv, mine, got, eb, terms, dmat, osend, isend, dsend,
                orb, irb, drb, oacc, iacc, dacc, ozb, izb, dzb, dots,
                wsem, lsem, ms, mr, zs, zr, ys, yr, ps, pr, xs, xr, hs, hr,
                rys, ryr, rzs, rzr, ds_, dr_):
    n, nd, tb, e, f, d = p.n, p.nd, p.tb, p.e, p.f, p.d
    slow, fast, m, h, tbp = p.slow, p.fast, p.m, p.h, p.tbp
    me = lax.axis_index("expert")
    dp = lax.axis_index("dp")
    a, b = me // fast, lax.rem(me, fast)
    chip, core = dp // 2, lax.rem(dp, 2)
    partner = {"dp": chip * 2 + 1 - core}
    spans = p.spans
    nc = len(spans)

    loads = [pltpu.make_async_copy(x, y, wsem.at[i]) for i, (x, y) in enumerate(((gw_h, gw), (uw_h, uw), (dw_h, dw)))]
    mine_in = [pltpu.make_async_copy(x, y.at[me], lsem.at[i]) for i, (x, y) in enumerate(((tok_h, tokb), (grad_h, gradb)))]
    routing = [pltpu.make_async_copy(x, y, lsem.at[2 + i]) for i, (x, y) in enumerate(((ids_h, ids), (wts_h, wts)))]
    for c in routing + mine_in + loads:
        c.start()
    for c in routing:
        c.wait()

    which = lax.broadcasted_iota(jnp.int32, (p.experts, tb), 0)
    w = jnp.zeros((p.experts, tb), F32)
    for k in range(p.top):
        w = w + jnp.where(which == ids[k:k + 1, :], wts[k:k + 1, :].astype(F32), 0.0)
    wown[...] = jnp.zeros_like(wown)
    wown[:, 0:tb] = w.astype(BF)
    wall[me] = wown[...]

    sem = pltpu.get_barrier_semaphore()
    for j in range(1, n):
        pl.semaphore_signal(sem, inc=1, device_id={"expert": lax.rem(me + j, n)}, device_id_type=MESH)
    for j in range(1, nd):
        pl.semaphore_signal(sem, inc=1, device_id={"dp": lax.rem(dp + j, nd)}, device_id_type=MESH)
    pl.semaphore_wait(sem, n - 1 + nd - 1)

    blocks, homes = (tokb, gradb), (tok_h, grad_h)

    def source(jz, jj):
        return flip(a, jz) * fast + lax.rem(b - jj + fast, fast)

    def meta(j):
        return remote(wown, wall.at[me], ms.at[j], mr.at[j], {"expert": lax.rem(me + j, n)})

    def zcopy(i, jz):
        return remote(homes[i], blocks[i].at[me], zs.at[i, jz], zr.at[i, jz], {"expert": flip(a, jz) * fast + b})

    def ycopy(i, jz, jj):
        blk = source(jz, 0)
        src = homes[i] if jz == 0 else blocks[i].at[blk]
        return remote(src, blocks[i].at[blk], ys.at[i, jz, jj], yr.at[i, jz, jj],
                      {"expert": a * fast + lax.rem(b + jj, fast)})

    def forward(i, jz):
        if jz:
            zcopy(i, jz).wait_recv()
        for jj in range(1, fast):
            ycopy(i, jz, jj).start()

    def settle(i, group, flat):
        for jz in group:
            for jj in range(fast):
                if jj:
                    ycopy(i, jz, jj).wait_recv()
                elif jz == 0:
                    mine_in[i].wait()
                at = p.place(jz, jj) * tbp
                flat[at:at + tb] = blocks[i][source(jz, jj)]

    for j in range(1, n):
        meta(j).start()
    head = p.early + p.late[:1]
    tail = p.late[1:]
    for jz in head:
        if jz:
            zcopy(0, jz).start()
    forward(0, 0)
    forward(1, 0)

    tokf[...] = jnp.zeros_like(tokf)
    gradf[...] = jnp.zeros_like(gradf)
    tl = p.tl
    lower = ((lax.broadcasted_iota(jnp.int32, (tl, tl), 0) < lax.broadcasted_iota(jnp.int32, (tl, tl), 1))
             & ((lax.broadcasted_iota(jnp.int32, (tl, tl), 0) < p.hb)
                == (lax.broadcasted_iota(jnp.int32, (tl, tl), 1) < p.hb)))
    lower = jnp.where(lower, 1.0, 0.0).astype(BF)

    for jz in p.early:
        if jz:
            forward(0, jz)
    for jz in tail:
        zcopy(0, jz).start()
    for jz in p.late[:1]:
        zcopy(1, jz).start()
        forward(0, jz)
    for j in range(1, n):
        meta(j).wait_recv()

    sub = lax.broadcasted_iota(jnp.int32, (p.experts, 128), 0)
    row = lax.broadcasted_iota(jnp.int32, (16, 128), 0)
    wl = jnp.zeros((16, tl), F32)
    for jz in p.zorder:
        for jj in range(fast):
            full = wall[source(jz, jj)].astype(F32)
            v = jnp.zeros((16, 128), F32)
            for i in range(e):
                v = jnp.where(row == i, jnp.sum(jnp.where(sub == me * e + i, full, 0.0), axis=0, keepdims=True), v)
            if tl > 128:
                v = jnp.concatenate([v, jnp.zeros((16, tl - 128), F32)], axis=1)
            at = p.place(jz, jj) * tbp
            wl = wl + (pltpu.roll(v, at, 1) if at else v)
    match = wl > 0.0
    rank = dotted(jnp.where(match, 1.0, 0.0).astype(BF), lower, 1, 0)
    lane = lax.broadcasted_iota(jnp.int32, (16, tl), 1)
    at_slot = jnp.where(match, jnp.where(lane < p.hb, rank, CAP - 1.0 - rank), -1.0)
    line = lax.broadcasted_iota(jnp.int32, (CAP, tl), 0).astype(F32)
    for i in range(e):
        pick = jnp.abs(line - at_slot[i:i + 1, :]) < 0.5
        one[i] = jnp.where(pick, 1.0, 0.0).astype(BF)
        scaled[i] = jnp.where(pick, wl[i:i + 1, :], 0.0).astype(BF)

    settle(0, p.early, tokf)

    def reach(cs):
        return spans[cs[0]][0], spans[cs[-1]][1]

    def take(table, flat, out, cs):
        for c in cs:
            s0, s1, l0, l1, _ = spans[c]
            for i in range(e):
                out[i, s0:s1] = dotted(table[i, s0:s1, l0:l1], flat[l0:l1], 1, 0).astype(BF)

    def product(k, i, cs):
        s0, s1 = reach(cs)
        left = (rows, rows, sgrad)[k]
        right = (gw, uw, dw)[k]
        return dotted(left[i, s0:s1], right[i], 1, 1)

    def pair(k, cs):
        s0, s1 = reach(cs)
        return remote(psend.at[k, :, s0:s1], precv.at[k, :, s0:s1], ps.at[k, cs[0]], pr.at[k, cs[0]], partner)

    def cross(k, c, j):
        s0, s1 = spans[c][:2]
        return remote(mine.at[k, :, s0:s1], got.at[k, j, :, s0:s1], xs.at[k, c, j], xr.at[k, c, j],
                      {"dp": lax.rem(chip + j, m) * 2 + core})

    def theirs(k, cs):
        s0, s1 = reach(cs)
        for u in range(h):
            psend[k, u, s0:s1] = product(k, (1 - core) * h + u, cs).astype(BF)
        pair(k, cs).start()

    def ours(k, cs):
        g0 = spans[cs[0]][0]
        part = [product(k, core * h + u, cs) for u in range(h)]
        pair(k, cs).wait_recv()
        for c in cs:
            s0, s1 = spans[c][:2]
            for u in range(h):
                mine[k, u, s0:s1] = (part[u][s0 - g0:s1 - g0] + precv[k, u, s0:s1].astype(F32)).astype(BF)
            for j in range(1, m):
                cross(k, c, j).start()

    def total(k, c, u):
        s0, s1 = spans[c][:2]
        v = mine[k, u, s0:s1].astype(F32)
        for j in range(1, m):
            v = v + got[k, j, u, s0:s1].astype(F32)
        return v

    def share(k, c):
        s0, s1 = spans[c][:2]
        full = (hid, gd, ud)[k]
        view = full.at[pl.ds(core * h, h), s0:s1]
        return remote(view, view, hs.at[k, c], hr.at[k, c], partner)

    def make_hidden(c):
        s0, s1 = spans[c][:2]
        for k in (0, 1):
            for j in range(1, m):
                cross(k, c, j).wait_recv()
        for u in range(h):
            gate, up = total(0, c, u), total(1, c, u)
            hid[core * h + u, s0:s1] = (gate * jax.nn.sigmoid(gate) * up).astype(BF)
        share(0, c).start()

    def make_delta(c):
        s0, s1 = spans[c][:2]
        for j in range(1, m):
            cross(2, c, j).wait_recv()
        for u in range(h):
            gate, up, hg = total(0, c, u), total(1, c, u), total(2, c, u)
            sig = jax.nn.sigmoid(gate)
            gd[core * h + u, s0:s1] = (hg * up * sig * (1.0 + gate * (1.0 - sig))).astype(BF)
            ud[core * h + u, s0:s1] = (hg * gate * sig).astype(BF)
        share(1, c).start()
        share(2, c).start()

    def back(table, i, s0, s1, l0, l1, x):
        return dotted(table[i, s0:s1, l0:l1], x, 0, 0)

    sends = (osend, isend, dsend)
    rbufs = (orb, irb, drb)
    accs = (oacc, iacc, dacc)
    zbufs = (ozb, izb, dzb)

    def ry(i, jz, jj):
        to = a * fast + lax.rem(b + jj, fast)
        return remote(sends[i].at[flip(a, jz) * fast + lax.rem(b + jj, fast)], rbufs[i].at[jz, jj],
                      rys.at[i, jz, jj], ryr.at[i, jz, jj], {"expert": to})

    def rz(i, jz):
        return remote(accs[i].at[jz], zbufs[i].at[jz], rzs.at[i, jz], rzr.at[i, jz],
                      {"expert": flip(a, jz) * fast + b})

    def reply(jz, jj):
        return flip(a, jz) * fast + lax.rem(b + jj, fast)

    def lanes_of(group):
        if group is p.early:
            return 0, p.half, 0
        return p.back, p.tl, p.hb - p.back

    def put(i, group, value, skip, c0, c1):
        for g, jz in enumerate(group):
            for jj in range(fast):
                at = skip + (g * fast + jj) * tbp
                sends[i][reply(jz, (fast - jj) % fast), :, c0:c1] = value[at:at + tb].astype(BF)

    db = 256 if d % 256 == 0 else d
    fb = 256 if f % 256 == 0 else f

    def expert_out(cs):
        s0, s1 = reach(cs)
        for i in range(e):
            dot = jnp.zeros((s1 - s0, 1), F32)
            for c0 in range(0, d, db):
                v = dotted(hid[i, s0:s1], dw[i, :, c0:c0 + db], 1, 0)
                eb[i, s0:s1, c0:c0 + db] = v.astype(BF)
                dot = dot + jnp.sum(v * grows[i, s0:s1, c0:c0 + db].astype(F32), axis=1, keepdims=True)
            at = lax.broadcasted_iota(jnp.int32, (s1 - s0, dmat.shape[2]), 1) == me * e + i
            dmat[i, s0:s1] = jnp.where(at, dot, 0.0).astype(BF)

    def row_terms(cs):
        s0, s1 = reach(cs)
        for i in range(e):
            for c0 in range(0, d, db):
                terms[i, s0:s1, c0:c0 + db] = (dotted(gd[i, s0:s1], gw[i, :, c0:c0 + db], 1, 0)
                                               + dotted(ud[i, s0:s1], uw[i, :, c0:c0 + db], 1, 0)).astype(BF)

    def send_sum(i, table, data, group):
        s0, s1 = (0, p.hi) if group is p.early else (p.lo, CAP)
        l0, l1, skip = lanes_of(group)
        for c0 in range(0, d, db):
            v = sum(back(table, x, s0, s1, l0, l1, data[x, s0:s1, c0:c0 + db]) for x in range(e))
            put(i, group, v, skip, c0, c0 + db)
        for jz in reversed(group):
            for jj in range(1, fast):
                ry(i, jz, jj).start()

    def send_dots(group):
        s0, s1 = (0, p.hi) if group is p.early else (p.lo, CAP)
        l0, l1, skip = lanes_of(group)
        v = sum(dotted(dmat[x, s0:s1], one[x, s0:s1, l0:l1], 0, 0) for x in range(e))
        v = v[:p.experts]
        width = l1 - l0
        for g, jz in enumerate(group):
            for jj in range(fast):
                at = skip + (g * fast + jj) * tbp
                sends[2][reply(jz, (fast - jj) % fast)] = (pltpu.roll(v, (width - at) % width, 1) if at else v)[:, :128].astype(BF)
        for jz in reversed(group):
            for jj in range(1, fast):
                ry(2, jz, jj).start()

    def pass_on(i, group):
        for jz in reversed(group):
            v = sends[i][flip(a, jz) * fast + b].astype(F32)
            for jj in range(1, fast):
                ry(i, jz, jj).wait_recv()
                v = v + rbufs[i][jz, jj].astype(F32)
            accs[i][jz] = v.astype(BF)
            if jz:
                rz(i, jz).start()

    def result(i):
        v = accs[i][0].astype(F32)
        for jz in range(1, slow):
            rz(i, jz).wait_recv()
            v = v + zbufs[i][jz].astype(F32)
        return v

    def share_recv(k, cs):
        for c in cs:
            share(k, c).wait_recv()

    def weight_grad(out, left, right, i):
        for c0 in range(0, f, fb):
            out[i, c0:c0 + fb] = dotted(left[i, :, c0:c0 + fb], right[i], 0, 0).astype(BF)

    first = [c for c in range(nc) if not spans[c][4]]
    rest = [c for c in range(nc) if spans[c][4]]
    every = list(range(nc))
    near = [c for c in every if spans[c][0] < p.hi]
    far = [c for c in every if spans[c][0] >= p.hi]
    done = [c for c in first if c in near]

    loads[0].wait()
    if first:
        take(one, tokf, rows, first)
        theirs(0, first)
        ours(0, first)
    for jz in tail:
        forward(0, jz)
    for jz in p.zorder:
        if jz and jz not in p.late[:1]:
            zcopy(1, jz).start()
    for jz in p.late[:1]:
        forward(1, jz)
    loads[1].wait()
    if first:
        theirs(1, first)
        ours(1, first)
    settle(0, p.late, tokf)
    if rest:
        take(one, tokf, rows, rest)
        theirs(0, rest)
        ours(0, rest)
    for jz in p.early:
        if jz:
            forward(1, jz)
    if rest:
        theirs(1, rest)
        ours(1, rest)
    for jz in tail:
        forward(1, jz)
    for c in done:
        make_hidden(c)
    loads[2].wait()
    settle(1, p.zorder, gradf)
    take(scaled, gradf, sgrad, every)
    theirs(2, every)
    take(one, gradf, grows, every)
    ours(2, every)
    for c in near:
        if c not in done:
            make_hidden(c)
    share_recv(0, near)
    expert_out(near)
    send_sum(0, scaled, eb, p.early)
    send_dots(p.early)
    for c in far:
        make_hidden(c)
    if far:
        share_recv(0, far)
        expert_out(far)
    if p.late:
        send_sum(0, scaled, eb, p.late)
        send_dots(p.late)
    for c in near:
        make_delta(c)
    for i in (0, 2):
        pass_on(i, p.early)
    for k in (1, 2):
        share_recv(k, near)
    row_terms(near)
    send_sum(1, one, terms, p.early)
    for c in far:
        make_delta(c)
    if far:
        for k in (1, 2):
            share_recv(k, far)
        row_terms(far)
    if p.late:
        send_sum(1, one, terms, p.late)
        for i in (0, 2):
            pass_on(i, p.late)
    for i in range(e):
        weight_grad(gate_o, gd, rows, i)
    pass_on(1, p.early)

    def across(j):
        return remote(dots.at[0], dots.at[j], ds_.at[j], dr_.at[j], {"dp": lax.rem(dp + j, nd)})

    dots[0] = result(2).astype(BF)
    for j in range(1, nd):
        across(j).start()
    for i in range(e):
        weight_grad(up_o, ud, rows, i)
    if p.late:
        pass_on(1, p.late)
    for i in range(e):
        weight_grad(down_o, hid, sgrad, i)
    layer_o[...] = result(0).astype(BF)
    v = dots[0].astype(F32)
    for j in range(1, nd):
        across(j).wait()
        v = v + dots[j].astype(F32)
    v = v[:, :tb]
    for k in range(p.top):
        rg_o[k:k + 1, :] = jnp.sum(jnp.where(which == ids[k:k + 1, :], v, 0.0), axis=0, keepdims=True)
    tgrad_o[...] = result(1).astype(BF)

    for j in range(1, n):
        meta(j).wait_send()
    for i in range(2):
        for jz in range(slow):
            if jz:
                zcopy(i, jz).wait_send()
            for jj in range(1, fast):
                ycopy(i, jz, jj).wait_send()
    for k in range(3):
        for c in range(nc):
            share(k, c).wait_send()
            for j in range(1, m):
                cross(k, c, j).wait_send()
    for k in (0, 1):
        for cs in (first, rest):
            if cs:
                pair(k, cs).wait_send()
    pair(2, every).wait_send()
    for i in range(3):
        for jz in range(slow):
            if jz:
                rz(i, jz).wait_send()
            for jj in range(1, fast):
                ry(i, jz, jj).wait_send()


def main_call(n, nd, tok, grad, ids, wts, gw, uw, dw):
    e, f, d = gw.shape
    tb, top = tok.shape[0], ids.shape[0]
    p = Plan(n, nd, tb, top, e, f, d)
    nc = len(p.spans)
    vm, dma = pltpu.VMEM, pltpu.SemaphoreType.DMA
    block, el = (tb, d), up_to(p.experts, 128)
    dot = (p.experts, 128)
    per_half = (p.h, CAP, f)
    return pl.pallas_call(
        functools.partial(main_kernel, p),
        out_shape=[vm((tb, d), BF), vm((tb, d), BF), vm((top, tb), F32)] + [vm((e, f, d), BF)] * 3,
        in_specs=[HBM] * 7,
        out_specs=[VM] * 6,
        scratch_shapes=[vm((top, tb), jnp.int32), vm((top, tb), BF)] + [vm((e, CAP, f), BF)] * 3 + [vm((e, CAP, d), BF)] * 2 + [vm((e, f, d), BF)] * 3 + [vm((n,) + block, BF)] * 2 + [vm((p.tl, d), BF)] * 2
        + [vm(dot, BF), vm((n,) + dot, BF)] + [vm((e, CAP, p.tl), BF)] * 2 + [vm((e, CAP, d), BF)]
        + [vm((3,) + per_half, BF)] * 3 + [vm((3, p.m) + per_half, BF)]
        + [vm((e, CAP, d), BF)] * 2 + [vm((e, CAP, el), BF)]
        + [vm((n,) + block, BF)] * 2 + [vm((n,) + dot, BF)]
        + [vm((p.slow, p.fast) + block, BF)] * 2 + [vm((p.slow, p.fast) + dot, BF)]
        + ([vm((p.slow,) + block, BF)] * 2 + [vm((p.slow,) + dot, BF)]) * 2
        + [vm((nd,) + dot, BF)]
        + [dma((3,)), dma((4,))] + [dma((n,))] * 2 + [dma((2, p.slow))] * 2 + [dma((2, p.slow, p.fast))] * 2
        + [dma((3, nc))] * 2 + [dma((3, nc, p.m))] * 2 + [dma((3, nc))] * 2
        + [dma((3, p.slow, p.fast))] * 2 + [dma((3, p.slow))] * 2 + [dma((nd,))] * 2,
        compiler_params=pltpu.CompilerParams(collective_id=0, has_side_effects=True, vmem_limit_bytes=44 << 20),
    )(*[pltpu.with_memory_space_constraint(x, pltpu.HBM) for x in (tok, grad, ids, wts, gw, uw, dw)])


def flush_kernel(k, *refs):
    ins, outs, sem = refs[:k], refs[k:2 * k], refs[2 * k]
    copies = [pltpu.make_async_copy(x, y, sem.at[i]) for i, (x, y) in enumerate(zip(ins, outs))]
    for c in copies:
        c.start()
    for c in copies:
        c.wait()


def flush(*arrays):
    k = len(arrays)
    return pl.pallas_call(
        functools.partial(flush_kernel, k),
        out_shape=[jax.ShapeDtypeStruct(x.shape, x.dtype) for x in arrays],
        in_specs=[VM] * k, out_specs=[ANY] * k,
        scratch_shapes=[pltpu.SemaphoreType.DMA((k,))],
        compiler_params=pltpu.CompilerParams(vmem_limit_bytes=4 << 20),
    )(*[pltpu.with_memory_space_constraint(x, pltpu.VMEM) for x in arrays])


def body(n, nd, tokens, expert_ids, routing_weights, gate_weight, up_weight, down_weight, out_grad):
    layer, tgrad, rg, gate_grad, up_grad, down_grad = flush(*main_call(
        n, nd, tokens, out_grad, expert_ids.T, routing_weights.T, gate_weight, up_weight, down_weight))
    return layer, tgrad, rg.T, gate_grad, up_grad, down_grad


def solution(mesh):
    n, nd = mesh.shape["expert"], mesh.shape["dp"]
    w = P("expert", None, "dp")
    x = P("expert", "dp")
    r = P("expert", None)
    return jax.shard_map(functools.partial(body, n, nd), mesh=mesh, in_specs=(x, r, r, w, w, w, x),
                         out_specs=(x, x, r, w, w, w), check_vma=False)
```

```python
import functools
import jax
import jax.numpy as jnp
from jax import lax
from jax.experimental import pallas as pl
from jax.experimental.pallas import tpu as pltpu
from jax.sharding import PartitionSpec as P

CAP = 240
F32 = jnp.float32
BF = jnp.bfloat16
VM = pl.BlockSpec(memory_space=pltpu.VMEM)
ANY = pl.BlockSpec(memory_space=pl.ANY)
HBM = pl.BlockSpec(memory_space=pltpu.HBM)
MESH = pl.DeviceIdType.MESH


def up_to(x, k):
    return (x + k - 1) // k * k


def factor(n):
    slow = 4 if n % 4 == 0 else 1
    return slow, n // slow


def flip(a, j):
    bit = 1
    while bit <= j:
        if j & bit:
            a = a + bit - 2 * bit * lax.rem(a // bit, 2)
        bit *= 2
    return a


def remote(src, dst, send, recv, where):
    return pltpu.make_async_remote_copy(
        src_ref=src, dst_ref=dst, send_sem=send, recv_sem=recv,
        device_id=where, device_id_type=MESH,
    )


def dotted(x, y, dx, dy):
    return lax.dot_general(x, y, (((dx,), (dy,)), ((), ())), preferred_element_type=F32)


class Plan:
    def __init__(self, n, nd, tb, top, e, f, d):
        self.n, self.nd, self.tb, self.top, self.e, self.f, self.d = n, nd, tb, top, e, f, d
        self.slow, self.fast = factor(n)
        self.m = nd // 2
        self.h = e // 2
        self.experts = n * e
        self.tbp = up_to(tb, 16)
        self.tl = up_to(n * self.tbp, 128)
        order = list(range(self.slow))
        self.zorder = order[0::2] + order[1::2]
        self.nz = max(1, self.slow // 2)
        self.early = self.zorder[:self.nz]
        self.late = self.zorder[self.nz:]
        self.hb = self.nz * self.fast * self.tbp
        n1 = self.nz * self.fast * tb
        n2 = n * tb - n1
        lo = max(0, CAP - n2) // 16 * 16
        hi = min(CAP, up_to(n1, 16))
        self.hi = hi
        spans = []
        half = up_to(self.hb, 128)
        back = self.hb // 128 * 128
        for s0, s1, l0, l1, needs_late in ((0, lo, 0, half, False), (lo, hi, 0, self.tl, True),
                                           (hi, CAP, back, self.tl, True)):
            if s1 > s0:
                spans.append((s0, s1, l0, l1, needs_late))
        self.spans = spans
        self.lo = lo
        self.half, self.back = half, back
        self.gs = (2 if d % 256 == 0 else 1, 1)
        self.q = 2 if d % 512 == 0 else 1
        self.qw = d // self.q
        self.first = [c for c in range(len(spans)) if not spans[c][4]]
        self.rest = [c for c in range(len(spans)) if spans[c][4]]
        self.slots = {}
        self.number()

    def number(self):
        nc, slow, fast, m = len(self.spans), self.slow, self.fast, self.m
        keys = [("load", i) for i in range(3)] + [("route", i) for i in range(2)]
        keys += [(k,) for k in ("meta send", "meta", "pair send", "cross send", "dots send", "dots")]
        for i in range(2):
            keys += [("own", i, g) for g in range(self.gs[i])] + [("z send", i), ("y send", i), ("share send", i)]
            for g in range(self.gs[i]):
                keys += [("z", i, jz, g) for jz in range(1, slow)]
                keys += [("y", i, jz, jj, g) for jz in range(slow) for jj in range(1, fast)]
            keys += [("share", i, c) for c in range(nc)]
        keys += [("pair", k, cs[0]) for k in (0, 1) for cs in (self.first, self.rest) if cs] + [("pair", 2, 0)]
        keys += [("cross", k, c, j) for k in range(3) for c in range(nc) for j in range(1, m)]
        for i in range(3):
            keys += [("ry send", i), ("rz send", i)]
            for q in range(self.q if i < 2 else 1):
                keys += [("ry", i, q, jz, jj) for jz in range(slow) for jj in range(1, fast)]
                keys += [("rz", i, q, jz) for jz in range(1, slow)]
        for key in keys:
            self.slots[key] = len(self.slots)

    def place(self, jz, jj):
        return self.zorder.index(jz) * self.fast + jj


def main_kernel(p, tok_h, grad_h, ids_h, wts_h, gw_h, uw_h, dw_h,
                layer_o, tgrad_o, rg_o, gate_o, up_o, down_o,
                ids, wts, hid, gud, rows, sgrad, gw, uw, dw, tokb, gradb, tokf, gradf, wown, wall, one, scaled, grows,
                psend, precv, mine, got, eb, terms, dmat, osend, isend, dsend,
                orb, irb, drb, oacc, iacc, dacc, ozb, izb, dzb, dots, sems):
    n, nd, tb, e, f, d = p.n, p.nd, p.tb, p.e, p.f, p.d
    slow, fast, m, h, tbp = p.slow, p.fast, p.m, p.h, p.tbp
    me = lax.axis_index("expert")
    dp = lax.axis_index("dp")
    a, b = me // fast, lax.rem(me, fast)
    chip, core = dp // 2, lax.rem(dp, 2)
    partner = {"dp": chip * 2 + 1 - core}
    spans = p.spans
    nc = len(spans)

    def at(*key):
        return sems.at[p.slots[key]]

    def drain(ref, *key):
        pltpu.make_async_copy(ref, ref, at(*key)).wait()

    gs, nq, qw = p.gs, p.q, p.qw

    def cols(i, g):
        return slice(g * (d // gs[i]), (g + 1) * (d // gs[i]))

    def strip(i, g):
        return (tok_h, grad_h)[i].at[:, cols(i, g)]

    sem = pltpu.get_barrier_semaphore()
    for j in range(1, n):
        pl.semaphore_signal(sem, inc=1, device_id={"expert": lax.rem(me + j, n)}, device_id_type=MESH)
    for j in range(1, nd):
        pl.semaphore_signal(sem, inc=1, device_id={"dp": lax.rem(dp + j, nd)}, device_id_type=MESH)
    loads = [pltpu.make_async_copy(x, y, at("load", i)) for i, (x, y) in enumerate(((gw_h, gw), (uw_h, uw), (dw_h, dw)))]
    mine_in = [[pltpu.make_async_copy(strip(i, g), y.at[me, g], at("own", i, g)) for g in range(gs[i])]
               for i, y in enumerate((tokb, gradb))]
    routing = [pltpu.make_async_copy(x, y, at("route", i)) for i, (x, y) in enumerate(((ids_h, ids), (wts_h, wts)))]
    for c in routing + mine_in[0] + loads[:2] + mine_in[1] + loads[2:]:
        c.start()
    pl.semaphore_wait(sem, n - 1 + nd - 1)

    blocks = (tokb, gradb)

    def source(jz, jj):
        return flip(a, jz) * fast + lax.rem(b - jj + fast, fast)

    def meta(j):
        return remote(wown, wall.at[me], at("meta send"), at("meta"), {"expert": lax.rem(me + j, n)})

    def zcopy(i, jz, g):
        return remote(strip(i, g), blocks[i].at[me, g], at("z send", i), at("z", i, jz, g),
                      {"expert": flip(a, jz) * fast + b})

    def ycopy(i, jz, jj, g):
        blk = source(jz, 0)
        src = strip(i, g) if jz == 0 else blocks[i].at[blk, g]
        return remote(src, blocks[i].at[blk, g], at("y send", i), at("y", i, jz, jj, g),
                      {"expert": a * fast + lax.rem(b + jj, fast)})

    def outward(i, jz):
        for g in range(gs[i]):
            zcopy(i, jz, g).start()

    def forward(i, jz):
        for g in range(gs[i]):
            if jz:
                zcopy(i, jz, g).wait_recv()
            for jj in range(1, fast):
                ycopy(i, jz, jj, g).start()

    def settle(i, group, flat):
        for jz in group:
            for jj in range(fast):
                row = p.place(jz, jj) * tbp
                for g in range(gs[i]):
                    if jj:
                        ycopy(i, jz, jj, g).wait_recv()
                    elif jz == 0:
                        mine_in[i][g].wait()
                    flat[row:row + tb, cols(i, g)] = blocks[i][source(jz, jj), g]

    head = [jz for jz in p.early + p.late if jz]
    for jz in head[:1]:
        outward(0, jz)
    forward(0, 0)

    for c in routing:
        c.wait()
    which = lax.broadcasted_iota(jnp.int32, (p.experts, tb), 0)
    w = jnp.zeros((p.experts, tb), F32)
    for k in range(p.top):
        w = w + jnp.where(which == ids[k:k + 1, :], wts[k:k + 1, :].astype(F32), 0.0)
    wown[...] = jnp.zeros_like(wown)
    wown[:, 0:tb] = w.astype(BF)
    wall[me] = wown[...]
    for j in range(1, n):
        meta(j).start()
    for jz in head[1:]:
        outward(0, jz)
    for jz in p.late[:1] + [jz for jz in head if jz not in p.late[:1]]:
        outward(1, jz)

    tokf[...] = jnp.zeros_like(tokf)
    gradf[...] = jnp.zeros_like(gradf)
    tl = p.tl
    lower = ((lax.broadcasted_iota(jnp.int32, (tl, tl), 0) < lax.broadcasted_iota(jnp.int32, (tl, tl), 1))
             & ((lax.broadcasted_iota(jnp.int32, (tl, tl), 0) < p.hb)
                == (lax.broadcasted_iota(jnp.int32, (tl, tl), 1) < p.hb)))
    lower = jnp.where(lower, 1.0, 0.0).astype(BF)

    tail = p.late[1:]
    for jz in p.early:
        if jz:
            forward(0, jz)
    for jz in p.late[:1]:
        forward(0, jz)
    forward(1, 0)
    drain(wall.at[0:n - 1], "meta")

    sub = lax.broadcasted_iota(jnp.int32, (p.experts, 128), 0)
    row = lax.broadcasted_iota(jnp.int32, (16, 128), 0)
    wl = jnp.zeros((16, tl), F32)
    for jz in p.zorder:
        for jj in range(fast):
            full = wall[source(jz, jj)].astype(F32)
            v = jnp.zeros((16, 128), F32)
            for i in range(e):
                v = jnp.where(row == i, jnp.sum(jnp.where(sub == me * e + i, full, 0.0), axis=0, keepdims=True), v)
            if tl > 128:
                v = jnp.concatenate([v, jnp.zeros((16, tl - 128), F32)], axis=1)
            to = p.place(jz, jj) * tbp
            wl = wl + (pltpu.roll(v, to, 1) if to else v)
    match = wl > 0.0
    rank = dotted(jnp.where(match, 1.0, 0.0).astype(BF), lower, 1, 0)
    lane = lax.broadcasted_iota(jnp.int32, (16, tl), 1)
    at_slot = jnp.where(match, jnp.where(lane < p.hb, rank, CAP - 1.0 - rank), -1.0)
    line = lax.broadcasted_iota(jnp.int32, (CAP, tl), 0).astype(F32)
    for i in range(e):
        pick = jnp.abs(line - at_slot[i:i + 1, :]) < 0.5
        one[i] = jnp.where(pick, 1.0, 0.0).astype(BF)
        scaled[i] = jnp.where(pick, wl[i:i + 1, :], 0.0).astype(BF)

    settle(0, p.early, tokf)

    def reach(cs):
        return spans[cs[0]][0], spans[cs[-1]][1]

    def take(table, flat, out, cs):
        for c in cs:
            s0, s1, l0, l1, _ = spans[c]
            for i in range(e):
                out[i, s0:s1] = dotted(table[i, s0:s1, l0:l1], flat[l0:l1], 1, 0).astype(BF)

    def product(k, i, cs):
        s0, s1 = reach(cs)
        left = (rows, rows, sgrad)[k]
        right = (gw, uw, dw)[k]
        return dotted(left[i, s0:s1], right[i], 1, 1)

    def pair(k, cs):
        s0, s1 = reach(cs)
        return remote(psend.at[k, :, s0:s1], precv.at[k, :, s0:s1], at("pair send"), at("pair", k, cs[0]), partner)

    def cross(k, c, j):
        s0, s1 = spans[c][:2]
        return remote(mine.at[k, :, s0:s1], got.at[k, j, :, s0:s1], at("cross send"), at("cross", k, c, j),
                      {"dp": lax.rem(chip + j, m) * 2 + core})

    def theirs(k, cs):
        s0, s1 = reach(cs)
        for u in range(h):
            psend[k, u, s0:s1] = product(k, (1 - core) * h + u, cs).astype(BF)
        pair(k, cs).start()

    def exchange(k, c):
        for j in range(1, m):
            cross(k, c, j).start()

    def ours(k, cs):
        g0 = spans[cs[0]][0]
        part = [product(k, core * h + u, cs) for u in range(h)]
        pair(k, cs).wait_recv()
        for c in cs:
            s0, s1 = spans[c][:2]
            for u in range(h):
                mine[k, u, s0:s1] = (part[u][s0 - g0:s1 - g0] + precv[k, u, s0:s1].astype(F32)).astype(BF)
            if k == 2 or c == cs[0]:
                exchange(k, c)

    def total(k, c, u):
        s0, s1 = spans[c][:2]
        v = mine[k, u, s0:s1].astype(F32)
        for j in range(1, m):
            v = v + got[k, j, u, s0:s1].astype(F32)
        return v

    def share(k, c):
        s0, s1 = spans[c][:2]
        mid = pl.ds(core * h, h)
        view = hid.at[mid, s0:s1] if k == 0 else gud.at[:, mid, s0:s1]
        return remote(view, view, at("share send", k), at("share", k, c), partner)

    def make_hidden(c):
        s0, s1 = spans[c][:2]
        for k in (0, 1):
            for j in range(1, m):
                cross(k, c, j).wait_recv()
        for u in range(h):
            gate, up = total(0, c, u), total(1, c, u)
            hid[core * h + u, s0:s1] = (gate * jax.nn.sigmoid(gate) * up).astype(BF)
        share(0, c).start()

    def make_delta(c):
        s0, s1 = spans[c][:2]
        for j in range(1, m):
            cross(2, c, j).wait_recv()
        for u in range(h):
            gate, up, hg = total(0, c, u), total(1, c, u), total(2, c, u)
            sig = jax.nn.sigmoid(gate)
            gud[0, core * h + u, s0:s1] = (hg * up * sig * (1.0 + gate * (1.0 - sig))).astype(BF)
            gud[1, core * h + u, s0:s1] = (hg * gate * sig).astype(BF)
        share(1, c).start()

    def back(table, i, s0, s1, l0, l1, x):
        return dotted(table[i, s0:s1, l0:l1], x, 0, 0)

    sends = (osend, isend, dsend)
    rbufs = (orb, irb, drb)
    accs = (oacc, iacc, dacc)
    zbufs = (ozb, izb, dzb)
    pieces = (nq, nq, 1)

    def ry(i, q, jz, jj):
        to = a * fast + lax.rem(b + jj, fast)
        return remote(sends[i].at[q, flip(a, jz) * fast + lax.rem(b + jj, fast)], rbufs[i].at[q, jz, jj],
                      at("ry send", i), at("ry", i, q, jz, jj), {"expert": to})

    def rz(i, q, jz):
        return remote(accs[i].at[q, jz], zbufs[i].at[q, jz], at("rz send", i), at("rz", i, q, jz),
                      {"expert": flip(a, jz) * fast + b})

    def reply(jz, jj):
        return flip(a, jz) * fast + lax.rem(b + jj, fast)

    def lanes_of(group):
        if group is p.early:
            return 0, p.half, 0
        return p.back, p.tl, p.hb - p.back

    fb = 256 if f % 256 == 0 else f

    def slots_of(group):
        return (0, p.hi) if group is p.early else (p.lo, CAP)

    def off(i, q, group):
        for jz in reversed(group):
            for jj in range(1, fast):
                ry(i, q, jz, jj).start()

    def send_piece(i, q, table, data, group):
        s0, s1 = slots_of(group)
        l0, l1, skip = lanes_of(group)
        v = sum(back(table, x, s0, s1, l0, l1, data[x, s0:s1, q * qw:(q + 1) * qw]) for x in range(e))
        for g, jz in enumerate(group):
            for jj in range(fast):
                row = skip + (g * fast + jj) * tbp
                sends[i][q, reply(jz, (fast - jj) % fast)] = v[row:row + tb].astype(BF)
        off(i, q, group)

    def out_part(cs, group):
        if cs:
            s0, s1 = reach(cs)
            dot = [jnp.zeros((s1 - s0, 1), F32) for _ in range(e)]
        for q in range(nq):
            c0, c1 = q * qw, (q + 1) * qw
            if cs:
                for i in range(e):
                    v = dotted(hid[i, s0:s1], dw[i, :, c0:c1], 1, 0)
                    eb[i, s0:s1, c0:c1] = v.astype(BF)
                    dot[i] = dot[i] + jnp.sum(v * grows[i, s0:s1, c0:c1].astype(F32), axis=1, keepdims=True)
            if group:
                send_piece(0, q, scaled, eb, group)
        if cs:
            for i in range(e):
                own = lax.broadcasted_iota(jnp.int32, (s1 - s0, dmat.shape[2]), 1) == me * e + i
                dmat[i, s0:s1] = jnp.where(own, dot[i], 0.0).astype(BF)
        if group:
            s0, s1 = slots_of(group)
            l0, l1, skip = lanes_of(group)
            v = sum(dotted(dmat[x, s0:s1], one[x, s0:s1, l0:l1], 0, 0) for x in range(e))[:p.experts]
            width = l1 - l0
            for g, jz in enumerate(group):
                for jj in range(fast):
                    row = skip + (g * fast + jj) * tbp
                    w = (pltpu.roll(v, (width - row) % width, 1) if row else v)[:, :128]
                    sends[2][0, reply(jz, (fast - jj) % fast)] = w.astype(BF)
            off(2, 0, group)

    def in_part(cs, group, q):
        c0, c1 = q * qw, (q + 1) * qw
        if cs:
            s0, s1 = reach(cs)
            for i in range(e):
                terms[i, s0:s1, c0:c1] = (dotted(gud[0, i, s0:s1], gw[i, :, c0:c1], 1, 0)
                                          + dotted(gud[1, i, s0:s1], uw[i, :, c0:c1], 1, 0)).astype(BF)
        if group:
            send_piece(1, q, one, terms, group)

    def pass_on(i, q, group):
        for jz in reversed(group):
            v = sends[i][q, flip(a, jz) * fast + b].astype(F32)
            for jj in range(1, fast):
                ry(i, q, jz, jj).wait_recv()
                v = v + rbufs[i][q, jz, jj].astype(F32)
            accs[i][q, jz] = v.astype(BF)
            if jz:
                rz(i, q, jz).start()

    def result(i, q):
        v = accs[i][q, 0].astype(F32)
        for jz in range(1, slow):
            rz(i, q, jz).wait_recv()
            v = v + zbufs[i][q, jz].astype(F32)
        return v

    def share_recv(k, cs):
        for c in cs:
            share(k, c).wait_recv()

    def weight_grad(out, left, right, i):
        for c0 in range(0, f, fb):
            out[i, c0:c0 + fb] = dotted(left[i, :, c0:c0 + fb], right[i], 0, 0).astype(BF)

    first, rest = p.first, p.rest
    every = list(range(nc))
    near = [c for c in every if spans[c][0] < p.hi]
    far = [c for c in every if spans[c][0] >= p.hi]
    done = [c for c in first if c in near]

    loads[0].wait()
    if first:
        take(one, tokf, rows, first)
        theirs(0, first)
        ours(0, first)
    for jz in tail:
        forward(0, jz)
    for jz in p.late[:1]:
        forward(1, jz)
    loads[1].wait()
    if first:
        theirs(1, first)
        ours(1, first)
    settle(0, p.late, tokf)
    for jz in p.early:
        if jz:
            forward(1, jz)
    if rest:
        take(one, tokf, rows, rest)
        theirs(0, rest)
    for jz in tail:
        forward(1, jz)
    if rest:
        ours(0, rest)
        theirs(1, rest)
        ours(1, rest)
        for c in rest[1:]:
            for k in (0, 1):
                exchange(k, c)
    for c in done:
        make_hidden(c)
    loads[2].wait()
    settle(1, p.zorder, gradf)
    take(scaled, gradf, sgrad, every)
    theirs(2, every)
    take(one, gradf, grows, every)
    ours(2, every)
    for c in near:
        if c not in done:
            make_hidden(c)
    share_recv(0, near)
    out_part(near, p.early)
    for c in far:
        make_hidden(c)
    pass_on(2, 0, p.early)
    for q in range(nq):
        pass_on(0, q, p.early)
    share_recv(0, far)
    out_part(far, p.late)
    for c in near[:1]:
        make_delta(c)
    weight_grad(down_o, hid, sgrad, 0)
    for c in near[1:]:
        make_delta(c)
    for i in range(1, e):
        weight_grad(down_o, hid, sgrad, i)
    share_recv(1, near)
    for q in range(nq):
        in_part(near, p.early, q)
    for c in far:
        make_delta(c)
    pass_on(2, 0, p.late)
    for q in range(nq):
        pass_on(0, q, p.late)
    share_recv(1, far)
    for q in range(nq):
        in_part(far, p.late, q)
        pass_on(1, q, p.early)
    jobs = [(gate_o, gud.at[0], rows, i) for i in range(e)] + [(up_o, gud.at[1], rows, i) for i in range(e)]

    def job():
        if jobs:
            weight_grad(*jobs.pop(0))

    def across(j):
        return remote(dots.at[0], dots.at[j], at("dots send"), at("dots"), {"dp": lax.rem(dp + j, nd)})

    dots[0] = result(2, 0).astype(BF)
    for j in range(1, nd):
        across(j).start()
    job()
    for q in range(nq):
        pass_on(1, q, p.late)
        if q < nq - 1:
            job()
    while jobs:
        job()
    drain(dots.at[0:nd - 1], "dots")
    v = dots[0].astype(F32)
    for j in range(1, nd):
        v = v + dots[j].astype(F32)
    v = v[:, :tb]
    for k in range(p.top):
        rg_o[k:k + 1, :] = jnp.sum(jnp.where(which == ids[k:k + 1, :], v, 0.0), axis=0, keepdims=True)
    for i, out in ((0, layer_o), (1, tgrad_o)):
        for q in range(nq):
            out[:, q * qw:(q + 1) * qw] = result(i, q).astype(BF)

    drain(wall.at[0:n - 1], "meta send")
    drain(dots.at[0:nd - 1], "dots send")
    for i in range(2):
        if slow > 1:
            drain(blocks[i].at[0:slow - 1], "z send", i)
        if fast > 1:
            drain(blocks[i].at[0:slow * (fast - 1)], "y send", i)
    drain(psend, "pair send")
    if m > 1:
        drain(got.at[:, 1:m], "cross send")
    drain(hid.at[0:h], "share send", 0)
    drain(gud.at[:, 0:h], "share send", 1)
    for i in range(3):
        if slow > 1:
            drain(accs[i].at[:, 0:slow - 1], "rz send", i)
        if fast > 1:
            drain(sends[i].at[:, 0:slow * (fast - 1)], "ry send", i)


def main_call(n, nd, tok, grad, ids, wts, gw, uw, dw):
    e, f, d = gw.shape
    tb, top = tok.shape[0], ids.shape[0]
    p = Plan(n, nd, tb, top, e, f, d)
    nc = len(p.spans)
    vm, dma = pltpu.VMEM, pltpu.SemaphoreType.DMA
    piece, el = (tb, p.qw), up_to(p.experts, 128)
    dot = (p.experts, 128)
    per_half = (p.h, CAP, f)
    return pl.pallas_call(
        functools.partial(main_kernel, p),
        out_shape=[vm((tb, d), BF), vm((tb, d), BF), vm((top, tb), F32)] + [vm((e, f, d), BF)] * 3,
        in_specs=[HBM] * 7,
        out_specs=[VM] * 6,
        scratch_shapes=[vm((top, tb), jnp.int32), vm((top, tb), BF)] + [vm((e, CAP, f), BF), vm((2, e, CAP, f), BF)] + [vm((e, CAP, d), BF)] * 2 + [vm((e, f, d), BF)] * 3 + [vm((n, g, tb, d // g), BF) for g in p.gs] + [vm((p.tl, d), BF)] * 2
        + [vm(dot, BF), vm((n,) + dot, BF)] + [vm((e, CAP, p.tl), BF)] * 2 + [vm((e, CAP, d), BF)]
        + [vm((3,) + per_half, BF)] * 3 + [vm((3, p.m) + per_half, BF)]
        + [vm((e, CAP, d), BF)] * 2 + [vm((e, CAP, el), BF)]
        + [vm((p.q, n) + piece, BF)] * 2 + [vm((1, n) + dot, BF)]
        + [vm((p.q, p.slow, p.fast) + piece, BF)] * 2 + [vm((1, p.slow, p.fast) + dot, BF)]
        + ([vm((p.q, p.slow) + piece, BF)] * 2 + [vm((1, p.slow) + dot, BF)]) * 2
        + [vm((nd,) + dot, BF)]
        + [dma((len(p.slots),))],
        compiler_params=pltpu.CompilerParams(collective_id=0, has_side_effects=True, vmem_limit_bytes=44 << 20),
    )(*[pltpu.with_memory_space_constraint(x, pltpu.HBM) for x in (tok, grad, ids, wts, gw, uw, dw)])


def flush_kernel(k, *refs):
    ins, outs, sem = refs[:k], refs[k:2 * k], refs[2 * k]
    copies = [pltpu.make_async_copy(x, y, sem.at[i]) for i, (x, y) in enumerate(zip(ins, outs))]
    for c in copies:
        c.start()
    for c in copies:
        c.wait()


def flush(*arrays):
    k = len(arrays)
    return pl.pallas_call(
        functools.partial(flush_kernel, k),
        out_shape=[jax.ShapeDtypeStruct(x.shape, x.dtype) for x in arrays],
        in_specs=[VM] * k, out_specs=[ANY] * k,
        scratch_shapes=[pltpu.SemaphoreType.DMA((k,))],
        compiler_params=pltpu.CompilerParams(vmem_limit_bytes=4 << 20),
    )(*[pltpu.with_memory_space_constraint(x, pltpu.VMEM) for x in arrays])


def body(n, nd, tokens, expert_ids, routing_weights, gate_weight, up_weight, down_weight, out_grad):
    layer, tgrad, rg, gate_grad, up_grad, down_grad = flush(*main_call(
        n, nd, tokens, out_grad, expert_ids.T, routing_weights.T, gate_weight, up_weight, down_weight))
    return layer, tgrad, rg.T, gate_grad, up_grad, down_grad


def solution(mesh):
    n, nd = mesh.shape["expert"], mesh.shape["dp"]
    w = P("expert", None, "dp")
    x = P("expert", "dp")
    r = P("expert", None)
    return jax.shard_map(functools.partial(body, n, nd), mesh=mesh, in_specs=(x, r, r, w, w, w, x),
                         out_specs=(x, x, r, w, w, w), check_vma=False)
```

```python
import functools
import jax
import jax.numpy as jnp
from jax import lax
from jax.experimental import pallas as pl
from jax.experimental.pallas import tpu as pltpu
from jax.sharding import PartitionSpec as P

CAP = 240
F32 = jnp.float32
BF = jnp.bfloat16
VM = pl.BlockSpec(memory_space=pltpu.VMEM)
ANY = pl.BlockSpec(memory_space=pl.ANY)
HBM = pl.BlockSpec(memory_space=pltpu.HBM)
MESH = pl.DeviceIdType.MESH


def up_to(x, k):
    return (x + k - 1) // k * k


def factor(n):
    slow = 4 if n % 4 == 0 else 1
    return slow, n // slow


def flip(a, j):
    bit = 1
    while bit <= j:
        if j & bit:
            a = a + bit - 2 * bit * lax.rem(a // bit, 2)
        bit *= 2
    return a


def remote(src, dst, send, recv, where):
    return pltpu.make_async_remote_copy(
        src_ref=src, dst_ref=dst, send_sem=send, recv_sem=recv,
        device_id=where, device_id_type=MESH,
    )


def dotted(x, y, dx, dy):
    return lax.dot_general(x, y, (((dx,), (dy,)), ((), ())), preferred_element_type=F32)


class Plan:
    def __init__(self, n, nd, tb, top, e, f, d):
        self.n, self.nd, self.tb, self.top, self.e, self.f, self.d = n, nd, tb, top, e, f, d
        self.slow, self.fast = factor(n)
        self.m = nd // 2
        self.h = e // 2
        self.experts = n * e
        self.tbp = up_to(tb, 16)
        self.tl = up_to(n * self.tbp, 128)
        order = list(range(self.slow))
        self.zorder = order[0::2] + order[1::2]
        self.nz = max(1, self.slow // 2)
        self.early = self.zorder[:self.nz]
        self.late = self.zorder[self.nz:]
        self.hb = self.nz * self.fast * self.tbp
        n1 = self.nz * self.fast * tb
        n2 = n * tb - n1
        lo = max(0, CAP - n2) // 16 * 16
        hi = min(CAP, up_to(n1, 16))
        self.hi = hi
        spans = []
        half = up_to(self.hb, 128)
        back = self.hb // 128 * 128
        for s0, s1, l0, l1, needs_late in ((0, lo, 0, half, False), (lo, hi, 0, self.tl, True),
                                           (hi, CAP, back, self.tl, True)):
            if s1 > s0:
                spans.append((s0, s1, l0, l1, needs_late))
        self.spans = spans
        self.lo = lo
        self.half, self.back = half, back
        self.gs = (2 if d % 256 == 0 else 1, 1)
        self.q = 2 if d % 512 == 0 else 1
        self.qw = d // self.q
        self.first = [c for c in range(len(spans)) if not spans[c][4]]
        self.rest = [c for c in range(len(spans)) if spans[c][4]]
        self.slots = {}
        self.number()

    def number(self):
        nc, slow, fast, m = len(self.spans), self.slow, self.fast, self.m
        keys = [("load", i) for i in range(3)] + [("route", i) for i in range(2)]
        keys += [(k,) for k in ("meta send", "meta", "pair send", "cross send", "dots send", "dots")]
        for i in range(2):
            keys += [("own", i, g) for g in range(self.gs[i])] + [("z send", i), ("y send", i), ("share send", i)]
            for g in range(self.gs[i]):
                keys += [("z", i, jz, g) for jz in range(1, slow)]
                keys += [("y", i, jz, jj, g) for jz in range(slow) for jj in range(1, fast)]
            keys += [("share", i, c) for c in range(nc)]
        keys += [("pair", k, cs[0]) for k in (0, 1) for cs in (self.first, self.rest) if cs] + [("pair", 2, 0)]
        keys += [("cross", k, c, j) for k in range(3) for c in range(nc) for j in range(1, m)]
        for i in range(3):
            keys += [("ry send", i), ("rz send", i)]
            for q in range(self.q if i < 2 else 1):
                keys += [("ry", i, q, jz, jj) for jz in range(slow) for jj in range(1, fast)]
                keys += [("rz", i, q, jz) for jz in range(1, slow)]
        for key in keys:
            self.slots[key] = len(self.slots)

    def place(self, jz, jj):
        return self.zorder.index(jz) * self.fast + jj


def main_kernel(p, tok_h, grad_h, ids_h, wts_h, gw_h, uw_h, dw_h,
                layer_o, tgrad_o, rg_o, gate_o, up_o, down_o,
                ids, wts, hid, gud, rows, sgrad, gw, uw, dw, tokb, gradb, tokf, gradf, wown, wall, one, scaled, grows,
                psend, precv, mine, got, eb, terms, dmat, osend, isend, dsend,
                orb, irb, drb, oacc, iacc, dacc, ozb, izb, dzb, dots, sems):
    n, nd, tb, e, f, d = p.n, p.nd, p.tb, p.e, p.f, p.d
    slow, fast, m, h, tbp = p.slow, p.fast, p.m, p.h, p.tbp
    me = lax.axis_index("expert")
    dp = lax.axis_index("dp")
    a, b = me // fast, lax.rem(me, fast)
    chip, core = dp // 2, lax.rem(dp, 2)
    partner = {"dp": chip * 2 + 1 - core}
    spans = p.spans
    nc = len(spans)

    def at(*key):
        return sems.at[p.slots[key]]

    def drain(ref, *key):
        pltpu.make_async_copy(ref, ref, at(*key)).wait()

    gs, nq, qw = p.gs, p.q, p.qw

    def cols(i, g):
        return slice(g * (d // gs[i]), (g + 1) * (d // gs[i]))

    def strip(i, g):
        return (tok_h, grad_h)[i].at[:, cols(i, g)]

    sem = pltpu.get_barrier_semaphore()
    for j in range(1, n):
        pl.semaphore_signal(sem, inc=1, device_id={"expert": lax.rem(me + j, n)}, device_id_type=MESH)
    for j in range(1, nd):
        pl.semaphore_signal(sem, inc=1, device_id={"dp": lax.rem(dp + j, nd)}, device_id_type=MESH)
    loads = [pltpu.make_async_copy(x, y, at("load", i)) for i, (x, y) in enumerate(((gw_h, gw), (uw_h, uw), (dw_h, dw)))]
    mine_in = [[pltpu.make_async_copy(strip(i, g), y.at[me, g], at("own", i, g)) for g in range(gs[i])]
               for i, y in enumerate((tokb, gradb))]
    routing = [pltpu.make_async_copy(x, y, at("route", i)) for i, (x, y) in enumerate(((ids_h, ids), (wts_h, wts)))]
    for c in routing + mine_in[0] + loads[:2] + mine_in[1] + loads[2:]:
        c.start()
    pl.semaphore_wait(sem, n - 1 + nd - 1)

    blocks = (tokb, gradb)

    def source(jz, jj):
        return flip(a, jz) * fast + lax.rem(b - jj + fast, fast)

    def meta(j):
        return remote(wown, wall.at[me], at("meta send"), at("meta"), {"expert": lax.rem(me + j, n)})

    def zcopy(i, jz, g):
        return remote(strip(i, g), blocks[i].at[me, g], at("z send", i), at("z", i, jz, g),
                      {"expert": flip(a, jz) * fast + b})

    def ycopy(i, jz, jj, g):
        blk = source(jz, 0)
        src = strip(i, g) if jz == 0 else blocks[i].at[blk, g]
        return remote(src, blocks[i].at[blk, g], at("y send", i), at("y", i, jz, jj, g),
                      {"expert": a * fast + lax.rem(b + jj, fast)})

    def outward(i, jz, some=None):
        for g in range(gs[i]) if some is None else some:
            zcopy(i, jz, g).start()

    def forward(i, jz, some=None):
        for g in range(gs[i]) if some is None else some:
            if jz:
                zcopy(i, jz, g).wait_recv()
            for jj in range(1, fast):
                ycopy(i, jz, jj, g).start()

    def settle(i, group, flat):
        for jz in group:
            for jj in range(fast):
                row = p.place(jz, jj) * tbp
                for g in range(gs[i]):
                    if jj:
                        ycopy(i, jz, jj, g).wait_recv()
                    elif jz == 0:
                        mine_in[i][g].wait()
                    flat[row:row + tb, cols(i, g)] = blocks[i][source(jz, jj), g]

    head = [jz for jz in p.early + p.late if jz]

    for c in routing:
        c.wait()
    which = lax.broadcasted_iota(jnp.int32, (p.experts, tb), 0)
    w = jnp.zeros((p.experts, tb), F32)
    for k in range(p.top):
        w = w + jnp.where(which == ids[k:k + 1, :], wts[k:k + 1, :].astype(F32), 0.0)
    wown[...] = jnp.zeros_like(wown)
    wown[:, 0:tb] = w.astype(BF)
    wall[me] = wown[...]
    for j in range(1, n):
        meta(j).start()
    for jz in head[:1]:
        outward(0, jz)
    forward(0, 0)
    for jz in head[1:]:
        outward(0, jz)
    for jz in p.late[:1] + [jz for jz in head if jz not in p.late[:1]]:
        outward(1, jz)

    tokf[...] = jnp.zeros_like(tokf)
    gradf[...] = jnp.zeros_like(gradf)
    tl = p.tl
    lower = ((lax.broadcasted_iota(jnp.int32, (tl, tl), 0) < lax.broadcasted_iota(jnp.int32, (tl, tl), 1))
             & ((lax.broadcasted_iota(jnp.int32, (tl, tl), 0) < p.hb)
                == (lax.broadcasted_iota(jnp.int32, (tl, tl), 1) < p.hb)))
    lower = jnp.where(lower, 1.0, 0.0).astype(BF)

    tail = p.late[1:]

    def routed():
        drain(wall.at[0:n - 1], "meta")

    routed()
    sub = lax.broadcasted_iota(jnp.int32, (p.experts, 128), 0)
    er = up_to(e, 8)
    row = lax.broadcasted_iota(jnp.int32, (er, 128), 0)
    wl = jnp.zeros((er, tl), F32)
    for jz in p.zorder:
        for jj in range(fast):
            full = wall[source(jz, jj)].astype(F32)
            v = jnp.zeros((er, 128), F32)
            for i in range(e):
                v = jnp.where(row == i, jnp.sum(jnp.where(sub == me * e + i, full, 0.0), axis=0, keepdims=True), v)
            if tl > 128:
                v = jnp.concatenate([v, jnp.zeros((er, tl - 128), F32)], axis=1)
            to = p.place(jz, jj) * tbp
            wl = wl + (pltpu.roll(v, to, 1) if to else v)
    match = wl > 0.0
    rank = dotted(jnp.where(match, 1.0, 0.0).astype(BF), lower, 1, 0)
    lane = lax.broadcasted_iota(jnp.int32, (er, tl), 1)
    at_slot = jnp.where(match, jnp.where(lane < p.hb, rank, CAP - 1.0 - rank), -1.0)
    settle(0, p.early[:1], tokf)
    for jz in p.early[1:]:
        forward(0, jz, [0])
    line = lax.broadcasted_iota(jnp.int32, (CAP, tl), 0).astype(F32)
    for i in range(e):
        pick = jnp.abs(line - at_slot[i:i + 1, :]) < 0.5
        one[i] = jnp.where(pick, 1.0, 0.0).astype(BF)

    for jz in p.early[1:]:
        forward(0, jz, range(1, gs[0]))
    for jz in p.late[:1]:
        forward(0, jz)
    forward(1, 0)
    settle(0, p.early[1:], tokf)

    def reach(cs):
        return spans[cs[0]][0], spans[cs[-1]][1]

    def take(table, flat, out, cs):
        for c in cs:
            s0, s1, l0, l1, _ = spans[c]
            for i in range(e):
                out[i, s0:s1] = dotted(table[i, s0:s1, l0:l1], flat[l0:l1], 1, 0).astype(BF)

    def product(k, i, cs):
        s0, s1 = reach(cs)
        left = (rows, rows, sgrad)[k]
        right = (gw, uw, dw)[k]
        return dotted(left[i, s0:s1], right[i], 1, 1)

    def pair(k, cs):
        s0, s1 = reach(cs)
        return remote(psend.at[k, :, s0:s1], precv.at[k, :, s0:s1], at("pair send"), at("pair", k, cs[0]), partner)

    def cross(k, c, j):
        s0, s1 = spans[c][:2]
        return remote(mine.at[k, :, s0:s1], got.at[k, j, :, s0:s1], at("cross send"), at("cross", k, c, j),
                      {"dp": lax.rem(chip + j, m) * 2 + core})

    def theirs(k, cs):
        s0, s1 = reach(cs)
        for u in range(h):
            psend[k, u, s0:s1] = product(k, (1 - core) * h + u, cs).astype(BF)
        pair(k, cs).start()

    def exchange(k, c):
        for j in range(1, m):
            cross(k, c, j).start()

    def ours(k, cs):
        g0 = spans[cs[0]][0]
        part = [product(k, core * h + u, cs) for u in range(h)]
        pair(k, cs).wait_recv()
        for c in cs:
            s0, s1 = spans[c][:2]
            for u in range(h):
                mine[k, u, s0:s1] = (part[u][s0 - g0:s1 - g0] + precv[k, u, s0:s1].astype(F32)).astype(BF)
            if k == 2 or c == cs[0]:
                exchange(k, c)

    def total(k, c, u):
        s0, s1 = spans[c][:2]
        v = mine[k, u, s0:s1].astype(F32)
        for j in range(1, m):
            v = v + got[k, j, u, s0:s1].astype(F32)
        return v

    def share(k, c):
        s0, s1 = spans[c][:2]
        mid = pl.ds(core * h, h)
        view = hid.at[mid, s0:s1] if k == 0 else gud.at[:, mid, s0:s1]
        return remote(view, view, at("share send", k), at("share", k, c), partner)

    def make_hidden(c):
        s0, s1 = spans[c][:2]
        for k in (0, 1):
            for j in range(1, m):
                cross(k, c, j).wait_recv()
        for u in range(h):
            gate, up = total(0, c, u), total(1, c, u)
            hid[core * h + u, s0:s1] = (gate * jax.nn.sigmoid(gate) * up).astype(BF)
        share(0, c).start()

    def make_delta(c):
        s0, s1 = spans[c][:2]
        for j in range(1, m):
            cross(2, c, j).wait_recv()
        for u in range(h):
            gate, up, hg = total(0, c, u), total(1, c, u), total(2, c, u)
            sig = jax.nn.sigmoid(gate)
            gud[0, core * h + u, s0:s1] = (hg * up * sig * (1.0 + gate * (1.0 - sig))).astype(BF)
            gud[1, core * h + u, s0:s1] = (hg * gate * sig).astype(BF)
        share(1, c).start()

    def back(table, i, s0, s1, l0, l1, x):
        return dotted(table[i, s0:s1, l0:l1], x, 0, 0)

    sends = (osend, isend, dsend)
    rbufs = (orb, irb, drb)
    accs = (oacc, iacc, dacc)
    zbufs = (ozb, izb, dzb)
    pieces = (nq, nq, 1)

    def ry(i, q, jz, jj):
        to = a * fast + lax.rem(b + jj, fast)
        return remote(sends[i].at[q, flip(a, jz) * fast + lax.rem(b + jj, fast)], rbufs[i].at[q, jz, jj],
                      at("ry send", i), at("ry", i, q, jz, jj), {"expert": to})

    def rz(i, q, jz):
        return remote(accs[i].at[q, jz], zbufs[i].at[q, jz], at("rz send", i), at("rz", i, q, jz),
                      {"expert": flip(a, jz) * fast + b})

    def reply(jz, jj):
        return flip(a, jz) * fast + lax.rem(b + jj, fast)

    def lanes_of(group):
        if group is p.early:
            return 0, p.half, 0
        return p.back, p.tl, p.hb - p.back

    fb = 256 if f % 256 == 0 else f
    fd = 256 if d % 256 == 0 else d

    def slots_of(group):
        return (0, p.hi) if group is p.early else (p.lo, CAP)

    def off(i, q, group):
        for jz in reversed(group):
            for jj in range(1, fast):
                ry(i, q, jz, jj).start()

    def send_piece(i, q, table, data, group):
        s0, s1 = slots_of(group)
        l0, l1, skip = lanes_of(group)
        v = sum(back(table, x, s0, s1, l0, l1, data[x, s0:s1, q * qw:(q + 1) * qw]) for x in range(e))
        for g, jz in enumerate(group):
            for jj in range(fast):
                row = skip + (g * fast + jj) * tbp
                sends[i][q, reply(jz, (fast - jj) % fast)] = v[row:row + tb].astype(BF)
        off(i, q, group)

    def share_recv(k, cs):
        for c in cs:
            share(k, c).wait_recv()

    owned = [core * h + u for u in range(h)]
    others = [(1 - core) * h + u for u in range(h)]

    def out_rows(cs, which_ones):
        s0, s1 = reach(cs)
        for i in which_ones:
            dot = jnp.zeros((s1 - s0, 1), F32)
            for c0 in range(0, d, fd):
                v = dotted(hid[i, s0:s1], dw[i, :, c0:c0 + fd], 1, 0)
                eb[i, s0:s1, c0:c0 + fd] = v.astype(BF)
                dot = dot + jnp.sum(v * grows[i, s0:s1, c0:c0 + fd].astype(F32), axis=1, keepdims=True)
            own = lax.broadcasted_iota(jnp.int32, (s1 - s0, dmat.shape[2]), 1) == me * e + i
            dmat[i, s0:s1] = jnp.where(own, dot, 0.0).astype(BF)

    def out_part(cs, group):
        if cs:
            out_rows(cs, owned)
            share_recv(0, cs)
            out_rows(cs, others)
        if not group:
            return
        for q in range(nq):
            send_piece(0, q, scaled, eb, group)
        s0, s1 = slots_of(group)
        l0, l1, skip = lanes_of(group)
        v = sum(dotted(dmat[x, s0:s1], one[x, s0:s1, l0:l1], 0, 0) for x in range(e))[:p.experts]
        width = l1 - l0
        for g, jz in enumerate(group):
            for jj in range(fast):
                row = skip + (g * fast + jj) * tbp
                w = (pltpu.roll(v, (width - row) % width, 1) if row else v)[:, :128]
                sends[2][0, reply(jz, (fast - jj) % fast)] = w.astype(BF)
        off(2, 0, group)

    def in_rows(cs, which_ones, q):
        s0, s1 = reach(cs)
        c0, c1 = q * qw, (q + 1) * qw
        for i in which_ones:
            terms[i, s0:s1, c0:c1] = (dotted(gud[0, i, s0:s1], gw[i, :, c0:c1], 1, 0)
                                      + dotted(gud[1, i, s0:s1], uw[i, :, c0:c1], 1, 0)).astype(BF)

    def in_first(cs):
        if cs:
            for q in range(nq):
                in_rows(cs, owned, q)
            share_recv(1, cs)

    def in_part(cs, group, q):
        if cs:
            in_rows(cs, others, q)
        if group:
            send_piece(1, q, one, terms, group)

    def pass_on(i, q, group):
        for jz in reversed(group):
            v = sends[i][q, flip(a, jz) * fast + b].astype(F32)
            for jj in range(1, fast):
                ry(i, q, jz, jj).wait_recv()
                v = v + rbufs[i][q, jz, jj].astype(F32)
            accs[i][q, jz] = v.astype(BF)
            if jz:
                rz(i, q, jz).start()

    def result(i, q):
        v = accs[i][q, 0].astype(F32)
        for jz in range(1, slow):
            rz(i, q, jz).wait_recv()
            v = v + zbufs[i][q, jz].astype(F32)
        return v

    def weight_grad(out, left, right, i):
        for c0 in range(0, f, fb):
            out[i, c0:c0 + fb] = dotted(left[i, :, c0:c0 + fb], right[i], 0, 0).astype(BF)

    first, rest = p.first, p.rest
    every = list(range(nc))
    near = [c for c in every if spans[c][0] < p.hi]
    far = [c for c in every if spans[c][0] >= p.hi]
    done = [c for c in first if c in near]

    loads[0].wait()
    loads[1].wait()
    if first:
        take(one, tokf, rows, first)
        theirs(0, first)
    for jz in tail:
        forward(0, jz)
    if first:
        ours(0, first)
        theirs(1, first)
    for jz in p.late[:1]:
        forward(1, jz)
    for i in range(e):
        scaled[i] = one[i] * wl[i:i + 1, :].astype(BF)
    if first:
        ours(1, first)
    settle(0, p.late, tokf)
    for jz in p.early:
        if jz:
            forward(1, jz)
    if rest:
        take(one, tokf, rows, rest)
        theirs(0, rest)
    for jz in tail:
        forward(1, jz)
    if rest:
        ours(0, rest)
        theirs(1, rest)
        ours(1, rest)
        for c in rest[1:]:
            for k in (0, 1):
                exchange(k, c)
    for c in done:
        make_hidden(c)
    loads[2].wait()
    settle(1, p.zorder, gradf)
    take(scaled, gradf, sgrad, every)
    theirs(2, every)
    take(one, gradf, grows, every)
    ours(2, every)
    for c in near:
        if c not in done:
            make_hidden(c)
    out_part(near, p.early)
    for c in far:
        make_hidden(c)
    out_part(far, p.late)
    pass_on(2, 0, p.early)
    for q in range(nq):
        pass_on(0, q, p.early)
    for c in near[:1]:
        make_delta(c)
    weight_grad(down_o, hid, sgrad, 0)
    for c in near[1:]:
        make_delta(c)
    for i in range(1, e):
        weight_grad(down_o, hid, sgrad, i)
    in_first(near)
    for q in range(nq):
        in_part(near, p.early, q)
        pass_on(0, q, p.late)
    for c in far:
        make_delta(c)
    pass_on(2, 0, p.late)
    in_first(far)
    for q in range(nq):
        in_part(far, p.late, q)
        pass_on(1, q, p.early)
    jobs = [(gate_o, gud.at[0], rows, i) for i in range(e)] + [(up_o, gud.at[1], rows, i) for i in range(e)]

    def job():
        if jobs:
            weight_grad(*jobs.pop(0))

    def across(j):
        return remote(dots.at[0], dots.at[j], at("dots send"), at("dots"), {"dp": lax.rem(dp + j, nd)})

    job()
    for q in range(nq):
        pass_on(1, q, p.late)
        if q == 0:
            dots[0] = result(2, 0).astype(BF)
            for j in range(1, nd):
                across(j).start()
        if q < nq - 1:
            job()
    while jobs:
        job()
    drain(dots.at[0:nd - 1], "dots")
    v = dots[0].astype(F32)
    for j in range(1, nd):
        v = v + dots[j].astype(F32)
    v = v[:, :tb]
    for k in range(p.top):
        rg_o[k:k + 1, :] = jnp.sum(jnp.where(which == ids[k:k + 1, :], v, 0.0), axis=0, keepdims=True)
    for i, out in ((0, layer_o), (1, tgrad_o)):
        for q in range(nq):
            out[:, q * qw:(q + 1) * qw] = result(i, q).astype(BF)

    drain(wall.at[0:n - 1], "meta send")
    drain(dots.at[0:nd - 1], "dots send")
    for i in range(2):
        if slow > 1:
            drain(blocks[i].at[0:slow - 1], "z send", i)
        if fast > 1:
            drain(blocks[i].at[0:slow * (fast - 1)], "y send", i)
    drain(psend, "pair send")
    if m > 1:
        drain(got.at[:, 1:m], "cross send")
    drain(hid.at[0:h], "share send", 0)
    drain(gud.at[:, 0:h], "share send", 1)
    for i in range(3):
        if slow > 1:
            drain(accs[i].at[:, 0:slow - 1], "rz send", i)
        if fast > 1:
            drain(sends[i].at[:, 0:slow * (fast - 1)], "ry send", i)


def main_call(n, nd, tok, grad, ids, wts, gw, uw, dw):
    e, f, d = gw.shape
    tb, top = tok.shape[0], ids.shape[0]
    p = Plan(n, nd, tb, top, e, f, d)
    nc = len(p.spans)
    vm, dma = pltpu.VMEM, pltpu.SemaphoreType.DMA
    piece, el = (tb, p.qw), up_to(p.experts, 128)
    dot = (p.experts, 128)
    per_half = (p.h, CAP, f)
    return pl.pallas_call(
        functools.partial(main_kernel, p),
        out_shape=[vm((tb, d), BF), vm((tb, d), BF), vm((top, tb), F32)] + [vm((e, f, d), BF)] * 3,
        in_specs=[HBM] * 7,
        out_specs=[VM] * 6,
        scratch_shapes=[vm((top, tb), jnp.int32), vm((top, tb), BF)] + [vm((e, CAP, f), BF), vm((2, e, CAP, f), BF)] + [vm((e, CAP, d), BF)] * 2 + [vm((e, f, d), BF)] * 3 + [vm((n, g, tb, d // g), BF) for g in p.gs] + [vm((p.tl, d), BF)] * 2
        + [vm(dot, BF), vm((n,) + dot, BF)] + [vm((e, CAP, p.tl), BF)] * 2 + [vm((e, CAP, d), BF)]
        + [vm((3,) + per_half, BF)] * 3 + [vm((3, p.m) + per_half, BF)]
        + [vm((e, CAP, d), BF)] * 2 + [vm((e, CAP, el), BF)]
        + [vm((p.q, n) + piece, BF)] * 2 + [vm((1, n) + dot, BF)]
        + [vm((p.q, p.slow, p.fast) + piece, BF)] * 2 + [vm((1, p.slow, p.fast) + dot, BF)]
        + ([vm((p.q, p.slow) + piece, BF)] * 2 + [vm((1, p.slow) + dot, BF)]) * 2
        + [vm((nd,) + dot, BF)]
        + [dma((len(p.slots),))],
        compiler_params=pltpu.CompilerParams(collective_id=0, has_side_effects=True, vmem_limit_bytes=44 << 20),
    )(*[pltpu.with_memory_space_constraint(x, pltpu.HBM) for x in (tok, grad, ids, wts, gw, uw, dw)])


def flush_kernel(k, *refs):
    ins, outs, sem = refs[:k], refs[k:2 * k], refs[2 * k]
    pairs = []
    for x, y in zip(ins, outs):
        if len(x.shape) == 3:
            half = x.shape[1] // 2
            for i in range(x.shape[0]):
                pairs += [(x.at[i, r:r + half], y.at[i, r:r + half]) for r in (0, half)]
        else:
            pairs.append((x, y))
    copies = [pltpu.make_async_copy(x, y, sem.at[i]) for i, (x, y) in enumerate(pairs)]
    for c in copies:
        c.start()
    for c in copies:
        c.wait()


def flush(*arrays):
    k = len(arrays)
    return pl.pallas_call(
        functools.partial(flush_kernel, k),
        out_shape=[jax.ShapeDtypeStruct(x.shape, x.dtype) for x in arrays],
        in_specs=[VM] * k, out_specs=[ANY] * k,
        scratch_shapes=[pltpu.SemaphoreType.DMA((sum(2 * x.shape[0] if x.ndim == 3 else 1 for x in arrays),))],
        compiler_params=pltpu.CompilerParams(vmem_limit_bytes=4 << 20),
    )(*[pltpu.with_memory_space_constraint(x, pltpu.VMEM) for x in arrays])


def body(n, nd, tokens, expert_ids, routing_weights, gate_weight, up_weight, down_weight, out_grad):
    layer, tgrad, rg, gate_grad, up_grad, down_grad = flush(*main_call(
        n, nd, tokens, out_grad, expert_ids.T, routing_weights.T, gate_weight, up_weight, down_weight))
    return layer, tgrad, rg.T, gate_grad, up_grad, down_grad


def solution(mesh):
    n, nd = mesh.shape["expert"], mesh.shape["dp"]
    w = P("expert", None, "dp")
    x = P("expert", "dp")
    r = P("expert", None)
    return jax.shard_map(functools.partial(body, n, nd), mesh=mesh, in_specs=(x, r, r, w, w, w, x),
                         out_specs=(x, x, r, w, w, w), check_vma=False)
```

```python
import functools
import jax
import jax.numpy as jnp
from jax import lax
from jax.experimental import pallas as pl
from jax.experimental.pallas import tpu as pltpu
from jax.sharding import PartitionSpec as P

CAP = 240
F32 = jnp.float32
BF = jnp.bfloat16
VM = pl.BlockSpec(memory_space=pltpu.VMEM)
ANY = pl.BlockSpec(memory_space=pl.ANY)
HBM = pl.BlockSpec(memory_space=pltpu.HBM)
MESH = pl.DeviceIdType.MESH


def up_to(x, k):
    return (x + k - 1) // k * k


def factor(n):
    slow = 4 if n % 4 == 0 else 1
    return slow, n // slow


def flip(a, j):
    bit = 1
    while bit <= j:
        if j & bit:
            a = a + bit - 2 * bit * lax.rem(a // bit, 2)
        bit *= 2
    return a


def remote(src, dst, send, recv, where):
    return pltpu.make_async_remote_copy(
        src_ref=src, dst_ref=dst, send_sem=send, recv_sem=recv,
        device_id=where, device_id_type=MESH,
    )


def dotted(x, y, dx, dy):
    return lax.dot_general(x, y, (((dx,), (dy,)), ((), ())), preferred_element_type=F32)


class Plan:
    def __init__(self, n, nd, tb, top, e, f, d):
        self.n, self.nd, self.tb, self.top, self.e, self.f, self.d = n, nd, tb, top, e, f, d
        self.slow, self.fast = factor(n)
        self.m = nd // 2
        self.h = e // 2
        self.experts = n * e
        self.tbp = up_to(tb, 16)
        self.tl = up_to(n * self.tbp, 128)
        order = list(range(self.slow))
        self.zorder = order[0::2] + order[1::2]
        self.nz = max(1, self.slow // 2)
        self.early = self.zorder[:self.nz]
        self.late = self.zorder[self.nz:]
        self.hb = self.nz * self.fast * self.tbp
        n1 = self.nz * self.fast * tb
        n2 = n * tb - n1
        lo = max(0, CAP - n2) // 16 * 16
        hi = min(CAP, up_to(n1, 16))
        self.hi = hi
        spans = []
        half = up_to(self.hb, 128)
        back = self.hb // 128 * 128
        for s0, s1, l0, l1, needs_late in ((0, lo, 0, half, False), (lo, hi, 0, self.tl, True),
                                           (hi, CAP, back, self.tl, True)):
            if s1 > s0:
                spans.append((s0, s1, l0, l1, needs_late))
        self.spans = spans
        self.lo = lo
        self.half, self.back = half, back
        self.gs = (2 if d % 256 == 0 else 1, 1)
        self.q = 2 if d % 512 == 0 else 1
        self.qw = d // self.q
        self.first = [c for c in range(len(spans)) if not spans[c][4]]
        self.rest = [c for c in range(len(spans)) if spans[c][4]]
        self.slots = {}
        self.number()

    def number(self):
        nc, slow, fast, m = len(self.spans), self.slow, self.fast, self.m
        keys = [("load", i) for i in range(3)] + [("route", i) for i in range(2)]
        keys += [(k,) for k in ("meta send", "meta", "pair send", "cross send", "dots send", "dots")]
        for i in range(2):
            keys += [("own", i, g) for g in range(self.gs[i])] + [("z send", i), ("y send", i), ("share send", i)]
            for g in range(self.gs[i]):
                keys += [("z", i, jz, g) for jz in range(1, slow)]
                keys += [("y", i, jz, jj, g) for jz in range(slow) for jj in range(1, fast)]
            keys += [("share", i, c) for c in range(nc)]
        keys += [("pair", k, cs[0]) for k in (0, 1) for cs in (self.first, self.rest) if cs] + [("pair", 2, 0)]
        keys += [("cross", k, c, j) for k in range(3) for c in range(nc) for j in range(1, m)]
        for i in range(3):
            keys += [("ry send", i), ("rz send", i)]
            for q in range(self.q if i < 2 else 1):
                keys += [("ry", i, q, jz, jj) for jz in range(slow) for jj in range(1, fast)]
                keys += [("rz", i, q, jz) for jz in range(1, slow)]
        for key in keys:
            self.slots[key] = len(self.slots)

    def place(self, jz, jj):
        return self.zorder.index(jz) * self.fast + jj


def main_kernel(p, tok_h, grad_h, ids_h, wts_h, gw_h, uw_h, dw_h,
                layer_o, tgrad_o, rg_o, gate_o, up_o, down_o,
                ids, wts, hid, gud, rows, sgrad, gw, uw, dw, tokb, gradb, tokf, gradf, wown, wall, one, scaled, grows,
                psend, precv, mine, got, eb, terms, dmat, osend, isend, dsend,
                orb, irb, drb, oacc, iacc, dacc, ozb, izb, dzb, dots, sems):
    n, nd, tb, e, f, d = p.n, p.nd, p.tb, p.e, p.f, p.d
    slow, fast, m, h, tbp = p.slow, p.fast, p.m, p.h, p.tbp
    me = lax.axis_index("expert")
    dp = lax.axis_index("dp")
    a, b = me // fast, lax.rem(me, fast)
    chip, core = dp // 2, lax.rem(dp, 2)
    partner = {"dp": chip * 2 + 1 - core}
    spans = p.spans
    nc = len(spans)

    def at(*key):
        return sems.at[p.slots[key]]

    def drain(ref, *key):
        pltpu.make_async_copy(ref, ref, at(*key)).wait()

    gs, nq, qw = p.gs, p.q, p.qw

    def cols(i, g):
        return slice(g * (d // gs[i]), (g + 1) * (d // gs[i]))

    def strip(i, g):
        return (tok_h, grad_h)[i].at[:, cols(i, g)]

    sem = pltpu.get_barrier_semaphore()
    for j in range(1, n):
        pl.semaphore_signal(sem, inc=1, device_id={"expert": lax.rem(me + j, n)}, device_id_type=MESH)
    for j in range(1, nd):
        pl.semaphore_signal(sem, inc=1, device_id={"dp": lax.rem(dp + j, nd)}, device_id_type=MESH)
    loads = [pltpu.make_async_copy(x, y, at("load", i)) for i, (x, y) in enumerate(((gw_h, gw), (uw_h, uw), (dw_h, dw)))]
    mine_in = [[pltpu.make_async_copy(strip(i, g), y.at[me, g], at("own", i, g)) for g in range(gs[i])]
               for i, y in enumerate((tokb, gradb))]
    routing = [pltpu.make_async_copy(x, y, at("route", i)) for i, (x, y) in enumerate(((ids_h, ids), (wts_h, wts)))]
    for c in routing:
        c.start()
    pl.semaphore_wait(sem, n - 1 + nd - 1)

    blocks = (tokb, gradb)

    def source(jz, jj):
        return flip(a, jz) * fast + lax.rem(b - jj + fast, fast)

    def meta(j):
        return remote(wown, wall.at[me], at("meta send"), at("meta"), {"expert": lax.rem(me + j, n)})

    def zcopy(i, jz, g):
        return remote(strip(i, g), blocks[i].at[me, g], at("z send", i), at("z", i, jz, g),
                      {"expert": flip(a, jz) * fast + b})

    def ycopy(i, jz, jj, g):
        blk = source(jz, 0)
        src = strip(i, g) if jz == 0 else blocks[i].at[blk, g]
        return remote(src, blocks[i].at[blk, g], at("y send", i), at("y", i, jz, jj, g),
                      {"expert": a * fast + lax.rem(b + jj, fast)})

    def outward(i, jz, some=None):
        for g in range(gs[i]) if some is None else some:
            zcopy(i, jz, g).start()

    def forward(i, jz, some=None):
        for g in range(gs[i]) if some is None else some:
            if jz:
                zcopy(i, jz, g).wait_recv()
            for jj in range(1, fast):
                ycopy(i, jz, jj, g).start()

    def settle(i, group, flat):
        for jz in group:
            for jj in range(fast):
                row = p.place(jz, jj) * tbp
                for g in range(gs[i]):
                    if jj:
                        ycopy(i, jz, jj, g).wait_recv()
                    elif jz == 0:
                        mine_in[i][g].wait()
                    flat[row:row + tb, cols(i, g)] = blocks[i][source(jz, jj), g]

    head = [jz for jz in p.early + p.late if jz]

    for c in routing:
        c.wait()
    which = lax.broadcasted_iota(jnp.int32, (p.experts, tb), 0)
    w = jnp.zeros((p.experts, tb), F32)
    for k in range(p.top):
        w = w + jnp.where(which == ids[k:k + 1, :], wts[k:k + 1, :].astype(F32), 0.0)
    wown[...] = jnp.zeros_like(wown)
    wown[:, 0:tb] = w.astype(BF)
    wall[me] = wown[...]
    for j in range(1, n):
        meta(j).start()
    for jz in head[:1]:
        outward(0, jz)
    forward(0, 0)
    for jz in head[1:]:
        outward(0, jz)
    for jz in p.late[:1] + [jz for jz in head if jz not in p.late[:1]]:
        outward(1, jz)

    for c in mine_in[0] + loads[:2] + mine_in[1] + loads[2:]:
        c.start()

    tokf[...] = jnp.zeros_like(tokf)
    gradf[...] = jnp.zeros_like(gradf)
    tl = p.tl
    lower = ((lax.broadcasted_iota(jnp.int32, (tl, tl), 0) < lax.broadcasted_iota(jnp.int32, (tl, tl), 1))
             & ((lax.broadcasted_iota(jnp.int32, (tl, tl), 0) < p.hb)
                == (lax.broadcasted_iota(jnp.int32, (tl, tl), 1) < p.hb)))
    lower = jnp.where(lower, 1.0, 0.0).astype(BF)

    tail = p.late[1:]

    def routed():
        drain(wall.at[0:n - 1], "meta")

    routed()
    sub = lax.broadcasted_iota(jnp.int32, (p.experts, 128), 0)
    er = up_to(e, 8)
    row = lax.broadcasted_iota(jnp.int32, (er, 128), 0)
    wl = jnp.zeros((er, tl), F32)
    for jz in p.zorder:
        for jj in range(fast):
            full = wall[source(jz, jj)].astype(F32)
            v = jnp.zeros((er, 128), F32)
            for i in range(e):
                v = jnp.where(row == i, jnp.sum(jnp.where(sub == me * e + i, full, 0.0), axis=0, keepdims=True), v)
            if tl > 128:
                v = jnp.concatenate([v, jnp.zeros((er, tl - 128), F32)], axis=1)
            to = p.place(jz, jj) * tbp
            wl = wl + (pltpu.roll(v, to, 1) if to else v)
    match = wl > 0.0
    rank = dotted(jnp.where(match, 1.0, 0.0).astype(BF), lower, 1, 0)
    lane = lax.broadcasted_iota(jnp.int32, (er, tl), 1)
    at_slot = jnp.where(match, jnp.where(lane < p.hb, rank, CAP - 1.0 - rank), -1.0)
    settle(0, p.early[:1], tokf)
    for jz in p.early[1:]:
        forward(0, jz, [0])
    line = lax.broadcasted_iota(jnp.int32, (CAP, tl), 0).astype(F32)
    for i in range(e):
        pick = jnp.abs(line - at_slot[i:i + 1, :]) < 0.5
        one[i] = jnp.where(pick, 1.0, 0.0).astype(BF)

    for jz in p.early[1:]:
        forward(0, jz, range(1, gs[0]))
    for jz in p.late[:1]:
        forward(0, jz)
    forward(1, 0)
    settle(0, p.early[1:], tokf)

    def reach(cs):
        return spans[cs[0]][0], spans[cs[-1]][1]

    def take(table, flat, out, cs):
        for c in cs:
            s0, s1, l0, l1, _ = spans[c]
            for i in range(e):
                out[i, s0:s1] = dotted(table[i, s0:s1, l0:l1], flat[l0:l1], 1, 0).astype(BF)

    def product(k, i, cs):
        s0, s1 = reach(cs)
        left = (rows, rows, sgrad)[k]
        right = (gw, uw, dw)[k]
        return dotted(left[i, s0:s1], right[i], 1, 1)

    def pair(k, cs):
        s0, s1 = reach(cs)
        return remote(psend.at[k, :, s0:s1], precv.at[k, :, s0:s1], at("pair send"), at("pair", k, cs[0]), partner)

    def cross(k, c, j):
        s0, s1 = spans[c][:2]
        return remote(mine.at[k, :, s0:s1], got.at[k, j, :, s0:s1], at("cross send"), at("cross", k, c, j),
                      {"dp": lax.rem(chip + j, m) * 2 + core})

    def theirs(k, cs):
        s0, s1 = reach(cs)
        for u in range(h):
            psend[k, u, s0:s1] = product(k, (1 - core) * h + u, cs).astype(BF)
        pair(k, cs).start()

    def exchange(k, c):
        for j in range(1, m):
            cross(k, c, j).start()

    def ours(k, cs):
        g0 = spans[cs[0]][0]
        part = [product(k, core * h + u, cs) for u in range(h)]
        pair(k, cs).wait_recv()
        for c in cs:
            s0, s1 = spans[c][:2]
            for u in range(h):
                mine[k, u, s0:s1] = (part[u][s0 - g0:s1 - g0] + precv[k, u, s0:s1].astype(F32)).astype(BF)
            if k == 2 or c == cs[0]:
                exchange(k, c)

    def total(k, c, u):
        s0, s1 = spans[c][:2]
        v = mine[k, u, s0:s1].astype(F32)
        for j in range(1, m):
            v = v + got[k, j, u, s0:s1].astype(F32)
        return v

    def share(k, c):
        s0, s1 = spans[c][:2]
        mid = pl.ds(core * h, h)
        view = hid.at[mid, s0:s1] if k == 0 else gud.at[:, mid, s0:s1]
        return remote(view, view, at("share send", k), at("share", k, c), partner)

    def make_hidden(c):
        s0, s1 = spans[c][:2]
        for k in (0, 1):
            for j in range(1, m):
                cross(k, c, j).wait_recv()
        for u in range(h):
            gate, up = total(0, c, u), total(1, c, u)
            hid[core * h + u, s0:s1] = (gate * jax.nn.sigmoid(gate) * up).astype(BF)
        share(0, c).start()

    def make_delta(c):
        s0, s1 = spans[c][:2]
        for j in range(1, m):
            cross(2, c, j).wait_recv()
        for u in range(h):
            gate, up, hg = total(0, c, u), total(1, c, u), total(2, c, u)
            sig = jax.nn.sigmoid(gate)
            gud[0, core * h + u, s0:s1] = (hg * up * sig * (1.0 + gate * (1.0 - sig))).astype(BF)
            gud[1, core * h + u, s0:s1] = (hg * gate * sig).astype(BF)
        share(1, c).start()

    def back(table, i, s0, s1, l0, l1, x):
        return dotted(table[i, s0:s1, l0:l1], x, 0, 0)

    sends = (osend, isend, dsend)
    rbufs = (orb, irb, drb)
    accs = (oacc, iacc, dacc)
    zbufs = (ozb, izb, dzb)
    pieces = (nq, nq, 1)

    def ry(i, q, jz, jj):
        to = a * fast + lax.rem(b + jj, fast)
        return remote(sends[i].at[q, flip(a, jz) * fast + lax.rem(b + jj, fast)], rbufs[i].at[q, jz, jj],
                      at("ry send", i), at("ry", i, q, jz, jj), {"expert": to})

    def rz(i, q, jz):
        return remote(accs[i].at[q, jz], zbufs[i].at[q, jz], at("rz send", i), at("rz", i, q, jz),
                      {"expert": flip(a, jz) * fast + b})

    def reply(jz, jj):
        return flip(a, jz) * fast + lax.rem(b + jj, fast)

    def lanes_of(group):
        if group is p.early:
            return 0, p.half, 0
        return p.back, p.tl, p.hb - p.back

    fb = 256 if f % 256 == 0 else f
    fd = 256 if d % 256 == 0 else d

    def slots_of(group):
        return (0, p.hi) if group is p.early else (p.lo, CAP)

    def off(i, q, group):
        for jz in reversed(group):
            for jj in range(1, fast):
                ry(i, q, jz, jj).start()

    def send_piece(i, q, table, data, group):
        s0, s1 = slots_of(group)
        l0, l1, skip = lanes_of(group)
        v = sum(back(table, x, s0, s1, l0, l1, data[x, s0:s1, q * qw:(q + 1) * qw]) for x in range(e))
        for g, jz in enumerate(group):
            for jj in range(fast):
                row = skip + (g * fast + jj) * tbp
                sends[i][q, reply(jz, (fast - jj) % fast)] = v[row:row + tb].astype(BF)
        off(i, q, group)

    def share_recv(k, cs):
        for c in cs:
            share(k, c).wait_recv()

    owned = [core * h + u for u in range(h)]
    others = [(1 - core) * h + u for u in range(h)]

    def out_rows(cs, which_ones):
        s0, s1 = reach(cs)
        for i in which_ones:
            dot = jnp.zeros((s1 - s0, 1), F32)
            for c0 in range(0, d, fd):
                v = dotted(hid[i, s0:s1], dw[i, :, c0:c0 + fd], 1, 0)
                eb[i, s0:s1, c0:c0 + fd] = v.astype(BF)
                dot = dot + jnp.sum(v * grows[i, s0:s1, c0:c0 + fd].astype(F32), axis=1, keepdims=True)
            own = lax.broadcasted_iota(jnp.int32, (s1 - s0, dmat.shape[2]), 1) == me * e + i
            dmat[i, s0:s1] = jnp.where(own, dot, 0.0).astype(BF)

    def out_part(cs, group):
        if cs:
            out_rows(cs, owned)
            share_recv(0, cs)
            out_rows(cs, others)
        if not group:
            return
        for q in range(nq):
            send_piece(0, q, scaled, eb, group)
        s0, s1 = slots_of(group)
        l0, l1, skip = lanes_of(group)
        v = sum(dotted(dmat[x, s0:s1], one[x, s0:s1, l0:l1], 0, 0) for x in range(e))[:p.experts]
        width = l1 - l0
        for g, jz in enumerate(group):
            for jj in range(fast):
                row = skip + (g * fast + jj) * tbp
                w = (pltpu.roll(v, (width - row) % width, 1) if row else v)[:, :128]
                sends[2][0, reply(jz, (fast - jj) % fast)] = w.astype(BF)
        off(2, 0, group)

    def in_rows(cs, which_ones, q):
        s0, s1 = reach(cs)
        c0, c1 = q * qw, (q + 1) * qw
        for i in which_ones:
            terms[i, s0:s1, c0:c1] = (dotted(gud[0, i, s0:s1], gw[i, :, c0:c1], 1, 0)
                                      + dotted(gud[1, i, s0:s1], uw[i, :, c0:c1], 1, 0)).astype(BF)

    def in_first(cs):
        if cs:
            for q in range(nq):
                in_rows(cs, owned, q)
            share_recv(1, cs)

    def in_part(cs, group, q):
        if cs:
            in_rows(cs, others, q)
        if group:
            send_piece(1, q, one, terms, group)

    def pass_on(i, q, group):
        for jz in reversed(group):
            v = sends[i][q, flip(a, jz) * fast + b].astype(F32)
            for jj in range(1, fast):
                ry(i, q, jz, jj).wait_recv()
                v = v + rbufs[i][q, jz, jj].astype(F32)
            accs[i][q, jz] = v.astype(BF)
            if jz:
                rz(i, q, jz).start()

    def result(i, q):
        v = accs[i][q, 0].astype(F32)
        for jz in range(1, slow):
            rz(i, q, jz).wait_recv()
            v = v + zbufs[i][q, jz].astype(F32)
        return v

    def weight_grad(out, left, right, i):
        for c0 in range(0, f, fb):
            out[i, c0:c0 + fb] = dotted(left[i, :, c0:c0 + fb], right[i], 0, 0).astype(BF)

    first, rest = p.first, p.rest
    every = list(range(nc))
    near = [c for c in every if spans[c][0] < p.hi]
    far = [c for c in every if spans[c][0] >= p.hi]
    done = [c for c in first if c in near]

    loads[0].wait()
    loads[1].wait()
    if first:
        take(one, tokf, rows, first)
        theirs(0, first)
    for jz in tail:
        forward(0, jz)
    if first:
        ours(0, first)
        theirs(1, first)
    for jz in p.late[:1]:
        forward(1, jz)
    for i in range(e):
        scaled[i] = one[i] * wl[i:i + 1, :].astype(BF)
    if first:
        ours(1, first)
    settle(0, p.late, tokf)
    for jz in p.early:
        if jz:
            forward(1, jz)
    if rest:
        take(one, tokf, rows, rest)
        theirs(0, rest)
    for jz in tail:
        forward(1, jz)
    if rest:
        ours(0, rest)
        theirs(1, rest)
        ours(1, rest)
        for c in rest[1:]:
            for k in (0, 1):
                exchange(k, c)
    for c in done:
        make_hidden(c)
    loads[2].wait()
    settle(1, p.zorder, gradf)
    take(scaled, gradf, sgrad, every)
    theirs(2, every)
    take(one, gradf, grows, every)
    ours(2, every)
    for c in near:
        if c not in done:
            make_hidden(c)
    out_part(near, p.early)
    for c in far:
        make_hidden(c)
    out_part(far, p.late)
    pass_on(2, 0, p.early)
    for q in range(nq):
        pass_on(0, q, p.early)
    for c in near[:1]:
        make_delta(c)
    weight_grad(down_o, hid, sgrad, 0)
    for c in near[1:]:
        make_delta(c)
    for i in range(1, e):
        weight_grad(down_o, hid, sgrad, i)
    in_first(near)
    for q in range(nq):
        in_part(near, p.early, q)
        pass_on(0, q, p.late)
    for c in far:
        make_delta(c)
    pass_on(2, 0, p.late)
    in_first(far)
    for q in range(nq):
        in_part(far, p.late, q)
        pass_on(1, q, p.early)
    jobs = [(gate_o, gud.at[0], rows, i) for i in range(e)] + [(up_o, gud.at[1], rows, i) for i in range(e)]

    def job():
        if jobs:
            weight_grad(*jobs.pop(0))

    def across(j):
        return remote(dots.at[0], dots.at[j], at("dots send"), at("dots"), {"dp": lax.rem(dp + j, nd)})

    job()
    for q in range(nq):
        pass_on(1, q, p.late)
        if q == 0:
            dots[0] = result(2, 0).astype(BF)
            for j in range(1, nd):
                across(j).start()
        if q < nq - 1:
            job()
    while jobs:
        job()
    drain(dots.at[0:nd - 1], "dots")
    v = dots[0].astype(F32)
    for j in range(1, nd):
        v = v + dots[j].astype(F32)
    v = v[:, :tb]
    for k in range(p.top):
        rg_o[k:k + 1, :] = jnp.sum(jnp.where(which == ids[k:k + 1, :], v, 0.0), axis=0, keepdims=True)
    for i, out in ((0, layer_o), (1, tgrad_o)):
        for q in range(nq):
            out[:, q * qw:(q + 1) * qw] = result(i, q).astype(BF)

    drain(wall.at[0:n - 1], "meta send")
    drain(dots.at[0:nd - 1], "dots send")
    for i in range(2):
        if slow > 1:
            drain(blocks[i].at[0:slow - 1], "z send", i)
        if fast > 1:
            drain(blocks[i].at[0:slow * (fast - 1)], "y send", i)
    drain(psend, "pair send")
    if m > 1:
        drain(got.at[:, 1:m], "cross send")
    drain(hid.at[0:h], "share send", 0)
    drain(gud.at[:, 0:h], "share send", 1)
    for i in range(3):
        if slow > 1:
            drain(accs[i].at[:, 0:slow - 1], "rz send", i)
        if fast > 1:
            drain(sends[i].at[:, 0:slow * (fast - 1)], "ry send", i)


def main_call(n, nd, tok, grad, ids, wts, gw, uw, dw):
    e, f, d = gw.shape
    tb, top = tok.shape[0], ids.shape[0]
    p = Plan(n, nd, tb, top, e, f, d)
    nc = len(p.spans)
    vm, dma = pltpu.VMEM, pltpu.SemaphoreType.DMA
    piece, el = (tb, p.qw), up_to(p.experts, 128)
    dot = (p.experts, 128)
    per_half = (p.h, CAP, f)
    return pl.pallas_call(
        functools.partial(main_kernel, p),
        out_shape=[vm((tb, d), BF), vm((tb, d), BF), vm((top, tb), F32)] + [vm((e, f, d), BF)] * 3,
        in_specs=[HBM] * 7,
        out_specs=[VM] * 6,
        scratch_shapes=[vm((top, tb), jnp.int32), vm((top, tb), BF)] + [vm((e, CAP, f), BF), vm((2, e, CAP, f), BF)] + [vm((e, CAP, d), BF)] * 2 + [vm((e, f, d), BF)] * 3 + [vm((n, g, tb, d // g), BF) for g in p.gs] + [vm((p.tl, d), BF)] * 2
        + [vm(dot, BF), vm((n,) + dot, BF)] + [vm((e, CAP, p.tl), BF)] * 2 + [vm((e, CAP, d), BF)]
        + [vm((3,) + per_half, BF)] * 3 + [vm((3, p.m) + per_half, BF)]
        + [vm((e, CAP, d), BF)] * 2 + [vm((e, CAP, el), BF)]
        + [vm((p.q, n) + piece, BF)] * 2 + [vm((1, n) + dot, BF)]
        + [vm((p.q, p.slow, p.fast) + piece, BF)] * 2 + [vm((1, p.slow, p.fast) + dot, BF)]
        + ([vm((p.q, p.slow) + piece, BF)] * 2 + [vm((1, p.slow) + dot, BF)]) * 2
        + [vm((nd,) + dot, BF)]
        + [dma((len(p.slots),))],
        compiler_params=pltpu.CompilerParams(collective_id=0, has_side_effects=True, vmem_limit_bytes=44 << 20),
    )(*[pltpu.with_memory_space_constraint(x, pltpu.HBM) for x in (tok, grad, ids, wts, gw, uw, dw)])


def flush_kernel(k, *refs):
    ins, outs, sem = refs[:k], refs[k:2 * k], refs[2 * k]
    pairs = []
    for x, y in zip(ins, outs):
        if len(x.shape) == 3:
            half = x.shape[1] // 2
            for i in range(x.shape[0]):
                pairs += [(x.at[i, r:r + half], y.at[i, r:r + half]) for r in (0, half)]
        else:
            pairs.append((x, y))
    copies = [pltpu.make_async_copy(x, y, sem.at[i]) for i, (x, y) in enumerate(pairs)]
    for c in copies:
        c.start()
    for c in copies:
        c.wait()


def flush(*arrays):
    k = len(arrays)
    return pl.pallas_call(
        functools.partial(flush_kernel, k),
        out_shape=[jax.ShapeDtypeStruct(x.shape, x.dtype) for x in arrays],
        in_specs=[VM] * k, out_specs=[ANY] * k,
        scratch_shapes=[pltpu.SemaphoreType.DMA((sum(2 * x.shape[0] if x.ndim == 3 else 1 for x in arrays),))],
        compiler_params=pltpu.CompilerParams(vmem_limit_bytes=4 << 20),
    )(*[pltpu.with_memory_space_constraint(x, pltpu.VMEM) for x in arrays])


def body(n, nd, tokens, expert_ids, routing_weights, gate_weight, up_weight, down_weight, out_grad):
    layer, tgrad, rg, gate_grad, up_grad, down_grad = flush(*main_call(
        n, nd, tokens, out_grad, expert_ids.T, routing_weights.T, gate_weight, up_weight, down_weight))
    return layer, tgrad, rg.T, gate_grad, up_grad, down_grad


def solution(mesh):
    n, nd = mesh.shape["expert"], mesh.shape["dp"]
    w = P("expert", None, "dp")
    x = P("expert", "dp")
    r = P("expert", None)
    return jax.shard_map(functools.partial(body, n, nd), mesh=mesh, in_specs=(x, r, r, w, w, w, x),
                         out_specs=(x, x, r, w, w, w), check_vma=False)
```
